512 devices in a mesh: ctx: 32 (over x_hi, z), tp: 16 (over x_lo, y, core).
Axes of the slice: x: 4 (x_hi: 2, x_lo: 2; x = x_hi * 2 + x_lo), y: 4, z: 16, core: 2. Of those that a mesh axis runs over, the one named last changes fastest.
Arguments:
- hidden_in: bfloat16 [16384, 4096], P('ctx', 'tp'), may hold values from -6 to 6
- norm_gain: bfloat16 [1, 4096], P(None, 'ctx'), may hold values from 0.25 to 1.75
- w_qkv: bfloat16 [1, 3, 4096, 2048], P(None, None, 'ctx', 'tp'), may hold values from -0.09375 to 0.09375
- w_out: bfloat16 [1, 2048, 4096], P(None, 'tp', 'ctx'), may hold values from -1 to 1
Outputs:
- hidden_out: bfloat16 [16384, 4096], P('ctx', 'tp')
The draws below stay inside these ranges and needn't reach their ends.
All inputs are finite; a program needn't handle non-finite values.
Results may differ from the reference program's by a relative error of at most 0.015.
Values may be sent and summed in bfloat16 or wider, within the bound.
No kernel may reach another device: no remote copies, remote signals or barrier semaphores. Data moves between devices by JAX's collectives and lax.ppermute only.
A program may use at most 64 MiB of HBM per device.

```python
import math
import jax
import jax.numpy as jnp
from jax import lax

D = 4096
HD = 128
LAYERS = 1
SEG = 512
HEADS = 16
TOKENS = 16384
N_CTX = 32


def shard_levels(rng, dims, split, least, high):
    def one(dim, shards_of):
        steps = jax.random.uniform(jax.random.fold_in(jax.random.fold_in(rng, 6), dim), (shards_of,), jnp.float32, least / len(split), high / len(split))
        return jnp.repeat(jnp.exp(steps), dims[dim] // shards_of).reshape((-1,) + (1,) * (len(dims) - dim - 1))

    factor_of = one(*split[0])
    for cut in split[1:]:
        factor_of = factor_of * one(*cut)
    return factor_of


def scatter_about(stream_key, shape, spread, reach, split=(), held_as=jnp.bfloat16):
    gain = shard_levels(stream_key, shape, split, -0.22, 0.18) if split else 1.0
    values = jax.random.normal(stream_key, shape, jnp.float32) * spread * gain
    return jnp.minimum(jnp.maximum(values, -reach), reach).astype(held_as)


def setup_inputs(seed: int = 0) -> dict:
    streams_of = jax.random.split(jax.random.key(seed), 5)
    hidden_in = scatter_about(streams_of[0], (TOKENS, D), 1.0, 6.0, ((0, 32), (1, 16)))
    norm_gain = jnp.clip(1.0 + 0.15 * jax.random.normal(streams_of[1], (LAYERS, D), jnp.float32), 0.25, 1.75).astype(jnp.bfloat16)
    w_qkv = scatter_about(streams_of[2], (LAYERS, 3, D, HEADS * HD), D ** -0.5, 0.09375, ((2, 32), (3, 16)))
    w_out = scatter_about(streams_of[3], (LAYERS, HEADS * HD, D), (HD // 4) ** -0.5, 1.0, ((1, 16), (2, 32)))
    return dict(hidden_in=hidden_in, norm_gain=norm_gain, w_qkv=w_qkv, w_out=w_out)


def normalize(hidden):
    values = hidden.astype(jnp.float32)
    return values * lax.rsqrt(lax.optimization_barrier(jnp.mean(values * values, axis=-1, keepdims=True)) + 1e-06)

def round_trip(values):
    return lax.optimization_barrier(values.astype(jnp.bfloat16)).astype(jnp.float32)

def attend(queries, key_rows, value_rows):
    heads = queries.shape[1] // HD
    shaped_q = queries.reshape(N_CTX, SEG, heads, HD)
    shaped_k = key_rows.reshape(N_CTX, SEG, heads, HD)
    shaped_v = value_rows.reshape(N_CTX, SEG, heads, HD)
    blank_seg = jnp.zeros((1, SEG, heads, HD), shaped_k.dtype)
    prev_k = jnp.concatenate([blank_seg, shaped_k[:-1]], axis=0)
    prev_v = jnp.concatenate([blank_seg, shaped_v[:-1]], axis=0)
    score_scale = 1.0 / math.sqrt(HD)
    row_ids = jnp.arange(SEG)[:, None]
    col_ids = jnp.arange(2 * SEG)[None, :]
    own_allowed = (col_ids >= SEG) & (col_ids - SEG <= row_ids)

    def one_segment(items):
        seg_q, seg_pk, seg_k, seg_pv, seg_v, seg_id = items
        keys_all = jnp.concatenate([seg_pk, seg_k], axis=0).astype(jnp.float32)
        values_all = jnp.concatenate([seg_pv, seg_v], axis=0).astype(jnp.float32)
        scores = jnp.einsum('qhd,khd->hqk', seg_q.astype(jnp.float32), keys_all) * score_scale
        allowed = own_allowed | (col_ids < SEG) & (seg_id > 0)
        exp_scores = jnp.where(allowed[None], jnp.exp(scores), 0.0)
        probs = round_trip(exp_scores / lax.optimization_barrier(jnp.sum(exp_scores, axis=-1, keepdims=True)))
        return jnp.einsum('hqk,khd->qhd', probs, values_all).astype(jnp.bfloat16)
    seg_ids = jnp.arange(N_CTX).astype(jnp.int32)
    attended = lax.map(one_segment, (shaped_q, prev_k, shaped_k, prev_v, shaped_v, seg_ids))
    return attended.reshape(N_CTX * SEG, heads * HD)

def reference(hidden_in, norm_gain, w_qkv, w_out):
    hidden = hidden_in
    for layer_index in range(LAYERS):
        normed = (normalize(hidden) * norm_gain[layer_index].astype(jnp.float32)).astype(jnp.bfloat16)
        queries = jnp.dot(normed, w_qkv[layer_index, 0], preferred_element_type=jnp.float32).astype(jnp.bfloat16)
        key_rows = jnp.dot(normed, w_qkv[layer_index, 1], preferred_element_type=jnp.float32).astype(jnp.bfloat16)
        value_rows = jnp.dot(normed, w_qkv[layer_index, 2], preferred_element_type=jnp.float32).astype(jnp.bfloat16)
        attended = attend(queries, key_rows, value_rows)
        out_weight = w_out[layer_index]

        def add_head(head_index, running):
            head_part = lax.dynamic_slice_in_dim(attended, head_index * HD, HD, 1)
            head_rows = lax.dynamic_slice_in_dim(out_weight, head_index * HD, HD, 0)
            return running + round_trip(jnp.dot(head_part, head_rows, preferred_element_type=jnp.float32))
        branch = lax.fori_loop(0, HEADS, add_head, jnp.zeros((N_CTX * SEG, D), jnp.float32))
        hidden = (hidden.astype(jnp.float32) + branch).astype(jnp.bfloat16)
    return hidden
```

```python
import math

import jax
import jax.numpy as jnp
from jax import lax
from jax.experimental import pallas as pl
from jax.experimental.pallas import tpu as pltpu
from jax.sharding import PartitionSpec as P

INTERPRET = False
AXES = ("ctx", "tp")
BF = jnp.bfloat16
F32 = jnp.float32
REV = [int(f"{p:04b}"[::-1], 2) for p in range(16)]


def pairs_of(target):
    pairs = []
    for src in range(512):
        ctx, tp = divmod(src, 16)
        a, z, b, y, k = ctx // 16, ctx % 16, tp // 8, tp // 2 % 4, tp % 2
        to = target(a, z, b, y, k)
        if to is not None:
            a, z, b, y, k = to
            pairs.append((src, (a * 16 + z % 16) * 16 + b * 8 + y % 4 * 2 + k))
    return pairs


def permute(value, target):
    return lax.ppermute(value, AXES, pairs_of(target))


def call(body, outs, scratch=(), flops=0, nbytes=1 << 20, vmem=24 << 20, scalars=True):
    def run(*args):
        specs = [pl.BlockSpec(memory_space=pltpu.VMEM) for _ in args]
        if scalars:
            specs[0] = pl.BlockSpec(memory_space=pltpu.SMEM)
        return pl.pallas_call(
            body,
            out_shape=outs,
            in_specs=specs,
            out_specs=jax.tree.map(lambda _: pl.BlockSpec(memory_space=pltpu.VMEM), outs),
            scratch_shapes=list(scratch),
            compiler_params=pltpu.CompilerParams(vmem_limit_bytes=vmem),
            cost_estimate=pl.CostEstimate(flops=flops, bytes_accessed=nbytes, transcendentals=0),
            interpret=INTERPRET,
        )(*args)

    return run


def shape(dims, dtype):
    return jax.ShapeDtypeStruct(dims, dtype)


def sign_of(k):
    return 1 - 2 * k


def gather_z(chunk):
    held = chunk
    for by in (8, 4, 2, 1):
        got = permute(held, lambda a, z, b, y, k: (a, z + sign_of(k) * by, b, y, k))
        if by > 1:
            held = jnp.concatenate([held, got], axis=0)
    return held, got


def source_z(z, k, p):
    return (z - sign_of(k) * REV[p] + 16) % 16


def project_body(pos, *refs):
    blocks, (w_lo, w_hi, own_ref, ssq_ref, send_ref, w_nat) = refs[:8], refs[8:]
    z, y, k = pos[1], pos[3], pos[4]
    rows = w_nat.shape[0] // 16
    for p in range(16):
        at = pl.multiple_of(source_z(z, k, p) * rows, rows)
        half = w_lo if p < 8 else w_hi
        w_nat[pl.ds(at, rows), :] = half[(p % 8) * rows : (p % 8 + 1) * rows, :]
    seg = own_ref.shape[0]
    tile = min(seg, 256)
    wide = own_ref.shape[1]
    for r in range(2 * seg // tile):
        acc = jnp.zeros((tile, wide), F32)
        ssq = jnp.zeros((tile, 1), F32)
        for i in range(8):
            yy = (y + i // 2) % 4
            kk = k if i % 2 == 0 else 1 - k
            at = pl.multiple_of((yy * 2 + kk) * 2 * rows, 2 * rows)
            block = blocks[i][r * tile : (r + 1) * tile, :]
            acc += jnp.dot(block, w_nat[pl.ds(at, 2 * rows), :], preferred_element_type=F32)
            wider = block.astype(F32)
            ssq += jnp.sum(wider * wider, axis=1, keepdims=True)
        at = r * tile % seg
        if r * tile < seg:
            own_ref[at : at + tile, :] = acc
            ssq_ref[at : at + tile, :] = jnp.broadcast_to(ssq, (tile, ssq_ref.shape[1]))
        else:
            send_ref[at : at + tile, :wide] = acc.astype(BF)
            lanes = send_ref.shape[1] - wide
            high = ssq.astype(BF).astype(F32)
            lane = lax.broadcasted_iota(jnp.int32, (tile, lanes), 1)
            both = jnp.where(lane < lanes // 2, high, ssq - high)
            send_ref[at : at + tile, wide:] = both.astype(BF)


def combine_body(own_ref, ssq_ref, got_ref, q_ref, kv_ref, *, features):
    hd = q_ref.shape[1]
    wide = 3 * hd
    lanes = got_ref.shape[1] - wide
    half = got_ref[:, wide:].astype(F32)
    ssq = ssq_ref[:, :1] + half[:, :1] + half[:, lanes // 2 : lanes // 2 + 1]
    scale = lax.rsqrt(ssq * (1.0 / features) + 1e-06)
    total = (own_ref[...] + got_ref[:, :wide].astype(F32)) * scale
    q_ref[...] = total[:, :hd].astype(BF)
    kv_ref[...] = total[:, hd:].astype(BF)


def scores_of(q, keys):
    hd = q.shape[1]
    return lax.dot_general(
        q, keys, (((1,), (1,)), ((), ())), preferred_element_type=F32
    ) * (1.0 / math.sqrt(hd))


def own_body(q_ref, kv_ref, e_ref, sum_ref):
    hd = q_ref.shape[1]
    scores = scores_of(q_ref[...], kv_ref[:, :hd])
    row = lax.broadcasted_iota(jnp.int32, scores.shape, 0)
    col = lax.broadcasted_iota(jnp.int32, scores.shape, 1)
    e = jnp.where(col <= row, jnp.exp(scores), 0.0)
    e_ref[...] = e
    sum_ref[...] = jnp.broadcast_to(jnp.sum(e, axis=1, keepdims=True), sum_ref.shape)


def attend_body(pos, q_ref, kv_ref, prev_ref, e_ref, sum_ref, out_ref):
    hd = q_ref.shape[1]
    e = jnp.exp(scores_of(q_ref[...], prev_ref[:, :hd]))
    first = pos[0] * 16 + pos[1] == 0
    e = jnp.where(jnp.full(e.shape, first), 0.0, e)
    total = sum_ref[:, :1] + jnp.sum(e, axis=1, keepdims=True)
    inverse = 1.0 / total
    out = jnp.dot((e_ref[...] * inverse).astype(BF), kv_ref[:, hd:], preferred_element_type=F32)
    out += jnp.dot((e * inverse).astype(BF), prev_ref[:, hd:], preferred_element_type=F32)
    out_ref[...] = out.astype(BF)


def output_body(pos, *refs):
    pieces, (w_lo, w_hi, hidden_ref, out_ref, w_nat) = refs[:8], refs[8:]
    a, z, b, y, k = pos[0], pos[1], pos[2], pos[3], pos[4]
    hd = w_nat.shape[3]
    for p in range(16):
        zz = source_z(z, k, p)
        e, o = zz % 2, (zz // 2 - 2 * y - k + 16) % 8
        half = w_lo if p < 8 else w_hi
        for s in range(2):
            at = (p % 8 * 2 + s) * hd
            w_nat[e, (a + s) % 2, o] = half[at : at + hd, :]
    total = hidden_ref[...].astype(F32)
    for i in range(8):
        yy = (y + i // 2) % 4
        kk = k if i % 2 == 0 else 1 - k
        o = yy * 2 + kk
        rows = [
            jnp.concatenate([w_nat[0, (b + s) % 2, o], w_nat[1, (b + s) % 2, o]], axis=1)
            for s in range(2)
        ]
        total += jnp.dot(pieces[i][...], jnp.concatenate(rows, axis=0), preferred_element_type=F32)
    out_ref[...] = total.astype(BF)


def swap_hi(a, z, b, y, k):
    return 1 - a, z, b, y, k


def swap_core(a, z, b, y, k):
    return a, z, b, y, 1 - k


def around(value):
    pieces = []
    for by in range(4):
        piece = value
        if by:
            piece = permute(value, lambda a, z, b, y, k: (a, z, b, y - by, k))
        pieces += [piece, permute(piece, swap_core)]
    return pieces


def per_device(hidden, norm_gain, w_qkv, w_out):
    seg, feats = hidden.shape
    hd = w_out.shape[1]
    ctx, tp = lax.axis_index("ctx"), lax.axis_index("tp")
    a, z, b, y, k = ctx // 16, ctx % 16, tp // 8, tp // 2 % 4, tp % 2
    pos = jnp.stack([a, z, b, y, k]).astype(jnp.int32)

    corner = {(0, 0): (0, 1), (0, 1): (1, 1), (1, 1): (1, 0), (1, 0): (0, 0)}
    turn = permute(hidden, lambda a, z, b, y, k: (*_at(corner, a, b, z), y, k))
    cross = permute(hidden, lambda a, z, b, y, k: (b, z, a, y, k) if a != b else None)
    own = jnp.where(a == b, hidden, turn)
    other = jnp.where(a == b, turn, cross)
    blocks = around(jnp.concatenate([own, other], axis=0))

    folded = w_qkv[0].astype(F32) * norm_gain[0].astype(F32)[None, :, None]
    chunk = jnp.concatenate([folded[0], folded[1], folded[2]], axis=1).astype(BF)
    w_lo, w_hi = gather_z(chunk)

    own_part, own_ssq, send = call(
        project_body,
        (shape((seg, 3 * hd), F32), shape((seg, hd), F32), shape((seg, 4 * hd), BF)),
        [pltpu.VMEM((16 * chunk.shape[0], 3 * hd), BF)],
        flops=4 * seg * 8 * feats * 3 * hd,
        nbytes=8 << 20,
    )(pos, *blocks, w_lo, w_hi)
    got = permute(send, swap_hi)
    q, kv = call(
        lambda *refs: combine_body(*refs, features=16 * feats),
        (shape((seg, hd), BF), shape((seg, 2 * hd), BF)),
        nbytes=2 << 20,
        scalars=False,
    )(own_part, own_ssq, got)
    prev = lax.ppermute(kv, "ctx", [(i, i + 1) for i in range(31)])
    e_own, sum_own = call(
        own_body,
        (shape((seg, seg), F32), shape((seg, hd), F32)),
        flops=2 * seg * seg * hd,
        nbytes=2 << 20,
        scalars=False,
    )(q, kv)
    attended = call(
        attend_body, shape((seg, hd), BF), flops=6 * seg * seg * hd, nbytes=2 << 20
    )(pos, q, kv, prev, e_own, sum_own)

    facing = permute(attended, lambda a, z, b, y, k: (a, z, 1 - b, y, k))
    pieces = around(jnp.concatenate([attended, facing], axis=1))

    piece = permute(
        w_out[0],
        lambda a, z, b, y, k: (b, z + 2 * (2 * y + k), a, z // 4, z // 2 % 2),
    )
    pair = jnp.concatenate([piece, permute(piece, swap_hi)], axis=0)
    o_lo, o_hi = gather_z(pair)
    return call(
        output_body,
        shape((seg, feats), BF),
        [pltpu.VMEM((2, 2, 8, hd, hd), BF)],
        flops=2 * seg * feats * 16 * hd,
        nbytes=4 << 20,
    )(pos, *pieces, o_lo, o_hi, hidden)


def _at(corner, a, b, z):
    to = corner[a, b]
    return to[0], z, to[1]


def solution(mesh):
    placed = (P("ctx", "tp"), P(None, "ctx"), P(None, None, "ctx", "tp"), P(None, "tp", "ctx"))
    return jax.shard_map(
        per_device, mesh=mesh, in_specs=placed, out_specs=P("ctx", "tp"), check_vma=False
    )
```

```python
import math

import jax
import jax.numpy as jnp
from jax import lax
from jax.experimental import pallas as pl
from jax.experimental.pallas import tpu as pltpu
from jax.sharding import PartitionSpec as P


INTERPRET = False
AXES = ("ctx", "tp")
BF = jnp.bfloat16
F32 = jnp.float32
REV = [int(f"{p:04b}"[::-1], 2) for p in range(16)]


def pairs_of(target):
    pairs = []
    for src in range(512):
        ctx, tp = divmod(src, 16)
        a, z, b, y, k = ctx // 16, ctx % 16, tp // 8, tp // 2 % 4, tp % 2
        to = target(a, z, b, y, k)
        if to is not None:
            a, z, b, y, k = to
            pairs.append((src, (a * 16 + z % 16) * 16 + b * 8 + y % 4 * 2 + k))
    return pairs


def permute(value, target):
    return lax.ppermute(value, AXES, pairs_of(target))


def call(body, outs, scratch=(), flops=0, nbytes=1 << 20, vmem=24 << 20, scalars=True):
    def run(*args):
        specs = [pl.BlockSpec(memory_space=pltpu.VMEM) for _ in args]
        if scalars:
            specs[0] = pl.BlockSpec(memory_space=pltpu.SMEM)
        return pl.pallas_call(
            body,
            out_shape=outs,
            in_specs=specs,
            out_specs=jax.tree.map(lambda _: pl.BlockSpec(memory_space=pltpu.VMEM), outs),
            scratch_shapes=list(scratch),
            compiler_params=pltpu.CompilerParams(vmem_limit_bytes=vmem),
            cost_estimate=pl.CostEstimate(flops=flops, bytes_accessed=nbytes, transcendentals=0),
            interpret=INTERPRET,
        )(*args)

    return run


def shape(dims, dtype):
    return jax.ShapeDtypeStruct(dims, dtype)


def sign_of(k):
    return 1 - 2 * k


def gather_z(chunk):
    held = chunk
    for by in (8, 4, 2, 1):
        got = permute(held, lambda a, z, b, y, k: (a, z + sign_of(k) * by, b, y, k))
        if by > 1:
            held = jnp.concatenate([held, got], axis=0)
    return held, got


def source_z(z, k, p):
    return (z - sign_of(k) * REV[p] + 16) % 16


def project_body(pos, *refs):
    blocks, (w_lo, w_hi, own_ref, ssq_ref, send_ref, out_w_ref, w_nat) = refs[:8], refs[8:]
    z, y, k = pos[1], pos[3], pos[4]
    rows = w_nat.shape[0] // 16
    wide = own_ref.shape[1]
    for p in range(16):
        at = pl.multiple_of(source_z(z, k, p) * rows, rows)
        half = w_lo if p < 8 else w_hi
        w_nat[pl.ds(at, rows), :] = half[(p % 8) * rows : (p % 8 + 1) * rows, :wide]
        out_w_ref[pl.ds(at, rows), :] = half[(p % 8) * rows : (p % 8 + 1) * rows, wide:]
    seg = own_ref.shape[0]
    tile = min(seg, 256)
    for r in range(2 * seg // tile):
        acc = jnp.zeros((tile, wide), F32)
        ssq = jnp.zeros((tile, 1), F32)
        for i in range(8):
            yy = (y + i // 2) % 4
            kk = k if i % 2 == 0 else 1 - k
            at = pl.multiple_of((yy * 2 + kk) * 2 * rows, 2 * rows)
            block = blocks[i][r * tile : (r + 1) * tile, :]
            acc += jnp.dot(block, w_nat[pl.ds(at, 2 * rows), :], preferred_element_type=F32)
            wider = block.astype(F32)
            ssq += jnp.sum(wider * wider, axis=1, keepdims=True)
        at = r * tile % seg
        if r * tile < seg:
            own_ref[at : at + tile, :] = acc
            ssq_ref[at : at + tile, :] = jnp.broadcast_to(ssq, (tile, ssq_ref.shape[1]))
        else:
            send_ref[at : at + tile, :wide] = acc.astype(BF)
            lanes = send_ref.shape[1] - wide
            high = ssq.astype(BF).astype(F32)
            lane = lax.broadcasted_iota(jnp.int32, (tile, lanes), 1)
            both = jnp.where(lane < lanes // 2, high, ssq - high)
            send_ref[at : at + tile, wide:] = both.astype(BF)


def combine_body(own_ref, ssq_ref, got_ref, q_ref, kv_ref, *, features):
    hd = q_ref.shape[1]
    wide = 3 * hd
    lanes = got_ref.shape[1] - wide
    half = got_ref[:, wide:].astype(F32)
    ssq = ssq_ref[:, :1] + half[:, :1] + half[:, lanes // 2 : lanes // 2 + 1]
    scale = lax.rsqrt(ssq * (1.0 / features) + 1e-06)
    total = (own_ref[...] + got_ref[:, :wide].astype(F32)) * scale
    q_ref[...] = total[:, :hd].astype(BF)
    kv_ref[...] = total[:, hd:].astype(BF)


def scores_of(q, keys):
    hd = q.shape[1]
    return lax.dot_general(
        q, keys, (((1,), (1,)), ((), ())), preferred_element_type=F32
    ) * (1.0 / math.sqrt(hd))


def own_body(q_ref, kv_ref, e_ref, sum_ref):
    hd = q_ref.shape[1]
    scores = scores_of(q_ref[...], kv_ref[:, :hd])
    row = lax.broadcasted_iota(jnp.int32, scores.shape, 0)
    col = lax.broadcasted_iota(jnp.int32, scores.shape, 1)
    e = jnp.where(col <= row, jnp.exp(scores), 0.0)
    e_ref[...] = e
    sum_ref[...] = jnp.broadcast_to(jnp.sum(e, axis=1, keepdims=True), sum_ref.shape)


def attend_body(pos, q_ref, kv_ref, prev_ref, e_ref, sum_ref, out_ref):
    hd = q_ref.shape[1]
    e = jnp.exp(scores_of(q_ref[...], prev_ref[:, :hd]))
    first = pos[0] * 16 + pos[1] == 0
    e = jnp.where(jnp.full(e.shape, first), 0.0, e)
    total = sum_ref[:, :1] + jnp.sum(e, axis=1, keepdims=True)
    inverse = 1.0 / total
    out = jnp.dot((e_ref[...] * inverse).astype(BF), kv_ref[:, hd:], preferred_element_type=F32)
    out += jnp.dot((e * inverse).astype(BF), prev_ref[:, hd:], preferred_element_type=F32)
    out_ref[...] = out.astype(BF)


def output_body(pos, *refs):
    pieces, (w_own, w_other, hidden_ref, out_ref, w_nat) = refs[:8], refs[8:]
    a, b, y, k = pos[0], pos[2], pos[3], pos[4]
    hd = w_nat.shape[2]
    w_nat[a] = w_own[...]
    w_nat[1 - a] = w_other[...]
    total = hidden_ref[...].astype(F32)
    for i in range(8):
        yy = (y + i // 2) % 4
        kk = k if i % 2 == 0 else 1 - k
        at = pl.multiple_of((yy * 2 + kk + 2 * y + k) % 8 * 2 * hd, 2 * hd)
        rows = []
        for head_b in (b, 1 - b):
            both = w_nat[head_b, pl.ds(at, 2 * hd), :]
            rows.append(jnp.concatenate([both[:hd], both[hd:]], axis=1))
        total += jnp.dot(pieces[i][...], jnp.concatenate(rows, axis=0), preferred_element_type=F32)
    out_ref[...] = total.astype(BF)


def swap_hi(a, z, b, y, k):
    return 1 - a, z, b, y, k


def swap_core(a, z, b, y, k):
    return a, z, b, y, 1 - k


def around(value):
    pieces = []
    for by in range(4):
        piece = value
        if by:
            piece = permute(value, lambda a, z, b, y, k: (a, z, b, y - by, k))
        pieces += [piece, permute(piece, swap_core)]
    return pieces


def layer(hidden, norm_gain, w_qkv, w_out):
    seg, feats = hidden.shape
    hd = w_out.shape[1]
    ctx, tp = lax.axis_index("ctx"), lax.axis_index("tp")
    a, z, b, y, k = ctx // 16, ctx % 16, tp // 8, tp // 2 % 4, tp % 2
    pos = jnp.stack([a, z, b, y, k]).astype(jnp.int32)

    corner = {(0, 0): (0, 1), (0, 1): (1, 1), (1, 1): (1, 0), (1, 0): (0, 0)}
    turn = permute(hidden, lambda a, z, b, y, k: (*_at(corner, a, b, z), y, k))
    cross = permute(hidden, lambda a, z, b, y, k: (b, z, a, y, k) if a != b else None)
    own = jnp.where(a == b, hidden, turn)
    other = jnp.where(a == b, turn, cross)
    blocks = around(jnp.concatenate([own, other], axis=0))

    piece = permute(w_out[0], lambda a, z, b, y, k: (b, z + 2 * (2 * y + k), a, z // 4, z // 2 % 2))
    folded = (w_qkv[0].astype(F32) * norm_gain[0].astype(F32)[None, :, None]).astype(BF)
    chunk = jnp.concatenate([folded[0], folded[1], folded[2], piece], axis=1)
    w_lo, w_hi = gather_z(chunk)

    own_part, own_ssq, send, out_w = call(
        project_body,
        (
            shape((seg, 3 * hd), F32),
            shape((seg, hd), F32),
            shape((seg, 4 * hd), BF),
            shape((16 * hd, hd), BF),
        ),
        [pltpu.VMEM((16 * hd, 3 * hd), BF)],
        flops=4 * seg * 8 * feats * 3 * hd,
        nbytes=8 << 20,
    )(pos, *blocks, w_lo, w_hi)
    got = permute(send, swap_hi)
    q, kv = call(
        lambda *refs: combine_body(*refs, features=16 * feats),
        (shape((seg, hd), BF), shape((seg, 2 * hd), BF)),
        nbytes=2 << 20,
        scalars=False,
    )(own_part, own_ssq, got)
    prev = lax.ppermute(kv, "ctx", [(i, i + 1) for i in range(31)])
    out_w_other = permute(out_w, swap_hi)
    e_own, sum_own = call(
        own_body,
        (shape((seg, seg), F32), shape((seg, hd), F32)),
        flops=2 * seg * seg * hd,
        nbytes=2 << 20,
        scalars=False,
    )(q, kv)
    attended = call(
        attend_body, shape((seg, hd), BF), flops=6 * seg * seg * hd, nbytes=2 << 20
    )(pos, q, kv, prev, e_own, sum_own)

    facing = permute(attended, lambda a, z, b, y, k: (a, z, 1 - b, y, k))
    pieces = around(jnp.concatenate([attended, facing], axis=1))
    return call(
        output_body,
        shape((seg, feats), BF),
        [pltpu.VMEM((2, 16 * hd, hd), BF)],
        flops=2 * seg * feats * 16 * hd,
        nbytes=4 << 20,
    )(pos, *pieces, out_w, out_w_other, hidden)


def _at(corner, a, b, z):
    to = corner[a, b]
    return to[0], z, to[1]


def solution(mesh):
    placed = (P("ctx", "tp"), P(None, "ctx"), P(None, None, "ctx", "tp"), P(None, "tp", "ctx"))
    return jax.shard_map(
        layer, mesh=mesh, in_specs=placed, out_specs=P("ctx", "tp"), check_vma=False
    )
```

```python
import math

import jax
import jax.numpy as jnp
from jax import lax
from jax.experimental import pallas as pl
from jax.experimental.pallas import tpu as pltpu
from jax.sharding import PartitionSpec as P


INTERPRET = False
AXES = ("ctx", "tp")
BF = jnp.bfloat16
F32 = jnp.float32
STEPS = ((0, -4, 4, 8), (2, 6), (-2, -6), (1, -3, 5, 9), (-1, -5, 3, 7))


def pairs_of(target):
    pairs = []
    for src in range(512):
        ctx, tp = divmod(src, 16)
        a, z, b, y, k = ctx // 16, ctx % 16, tp // 8, tp // 2 % 4, tp % 2
        to = target(a, z, b, y, k)
        if to is not None:
            a, z, b, y, k = to
            pairs.append((src, (a * 16 + z % 16) * 16 + b * 8 + y % 4 * 2 + k))
    return pairs


def permute(value, target):
    return lax.ppermute(value, AXES, pairs_of(target))


def call(body, outs, scratch=(), flops=0, nbytes=1 << 20, vmem=24 << 20, scalars=True):
    def run(*args):
        specs = [pl.BlockSpec(memory_space=pltpu.VMEM) for _ in args]
        if scalars:
            specs[0] = pl.BlockSpec(memory_space=pltpu.SMEM)
        return pl.pallas_call(
            body,
            out_shape=outs,
            in_specs=specs,
            out_specs=jax.tree.map(lambda _: pl.BlockSpec(memory_space=pltpu.VMEM), outs),
            scratch_shapes=list(scratch),
            compiler_params=pltpu.CompilerParams(vmem_limit_bytes=vmem),
            cost_estimate=pl.CostEstimate(flops=flops, bytes_accessed=nbytes, transcendentals=0),
            interpret=INTERPRET,
        )(*args)

    return run


def shape(dims, dtype):
    return jax.ShapeDtypeStruct(dims, dtype)


def place(pos):
    ctx, tp = pos[0], pos[1]
    return ctx >> 4, ctx & 15, tp >> 3, (tp >> 1) & 3, tp & 1


def gather_z(chunk, core):
    def move(value, by):
        return permute(value, lambda a, z, b, y, k: (a, z + by, b, y, k))

    up4 = move(chunk, 4)
    down4 = move(chunk, -4)
    relay = permute(
        jnp.where(core == 0, down4, up4), lambda a, z, b, y, k: (a, z + (4 if k else 12), b, y, k)
    )
    down2 = move(jnp.concatenate([chunk, down4], axis=0), -2)
    up2 = move(jnp.concatenate([chunk, up4], axis=0), 2)
    held = jnp.concatenate([chunk, up4, down4, relay], axis=0)
    down1 = move(held, -1)
    up1 = move(held, 1)
    return held, down2, up2, down1, up1


def project_rows(pos, blocks, weights, first, seg):
    _, _, _, y, k = place(pos)
    rows = weights.shape[0] // 16
    tile = min(seg, 256)
    for r in range(0, seg, tile):
        acc = jnp.zeros((tile, weights.shape[1]), F32)
        ssq = jnp.zeros((tile, 1), F32)
        for i in range(8):
            yy = (y + i // 2) & 3
            kk = k if i % 2 == 0 else 1 - k
            at = pl.multiple_of((yy * 2 + kk) * 2 * rows, 2 * rows)
            block = blocks[i][first + r : first + r + tile, :]
            acc += jnp.dot(block, weights[pl.ds(at, 2 * rows), :], preferred_element_type=F32)
            wider = block.astype(F32)
            ssq += jnp.sum(wider * wider, axis=1, keepdims=True)
        yield slice(r, r + tile), acc, ssq


def project_other_body(pos, *refs):
    blocks, parts, (send_ref, w_ref, out_w_ref) = refs[:8], refs[8:13], refs[13:]
    _, z, _, _, _ = place(pos)
    rows = w_ref.shape[0] // 16
    seg = send_ref.shape[0]
    wide = w_ref.shape[1]
    for part, steps in zip(parts, STEPS):
        for i, step in enumerate(steps):
            at = pl.multiple_of(((z + step + 16) & 15) * rows, rows)
            w_ref[pl.ds(at, rows), :] = part[i * rows : (i + 1) * rows, :wide]
            out_w_ref[pl.ds(at, rows), :] = part[i * rows : (i + 1) * rows, wide:]
    lanes = send_ref.shape[1] - wide
    for at, acc, ssq in project_rows(pos, blocks, w_ref, seg, seg):
        send_ref[at, :wide] = acc.astype(BF)
        high = ssq.astype(BF).astype(F32)
        lane = lax.broadcasted_iota(jnp.int32, (ssq.shape[0], lanes), 1)
        send_ref[at, wide:] = jnp.where(lane < lanes // 2, high, ssq - high).astype(BF)


def project_own_body(pos, *refs):
    blocks, (w_ref, own_ref, ssq_ref) = refs[:8], refs[8:]
    for at, acc, ssq in project_rows(pos, blocks, w_ref, 0, own_ref.shape[0]):
        own_ref[at, :] = acc
        ssq_ref[at, :] = jnp.broadcast_to(ssq, (ssq.shape[0], ssq_ref.shape[1]))


def combine_body(own_ref, ssq_ref, got_ref, q_ref, kv_ref, *, features):
    hd = q_ref.shape[1]
    wide = 3 * hd
    lanes = got_ref.shape[1] - wide
    half = got_ref[:, wide:].astype(F32)
    ssq = ssq_ref[:, :1] + half[:, :1] + half[:, lanes // 2 : lanes // 2 + 1]
    scale = lax.rsqrt(ssq * (1.0 / features) + 1e-06)
    total = (own_ref[...] + got_ref[:, :wide].astype(F32)) * scale
    q_ref[...] = total[:, :hd].astype(BF)
    kv_ref[...] = total[:, hd:].astype(BF)


def scores_of(q, keys):
    hd = q.shape[1]
    return lax.dot_general(
        q, keys, (((1,), (1,)), ((), ())), preferred_element_type=F32
    ) * (1.0 / math.sqrt(hd))


def own_body(q_ref, kv_ref, e_ref, sum_ref):
    hd = q_ref.shape[1]
    scores = scores_of(q_ref[...], kv_ref[:, :hd])
    row = lax.broadcasted_iota(jnp.int32, scores.shape, 0)
    col = lax.broadcasted_iota(jnp.int32, scores.shape, 1)
    e = jnp.where(col <= row, jnp.exp(scores), 0.0)
    e_ref[...] = e
    sum_ref[...] = jnp.broadcast_to(jnp.sum(e, axis=1, keepdims=True), sum_ref.shape)


def attend_body(pos, q_ref, kv_ref, prev_ref, e_ref, sum_ref, out_ref):
    hd = q_ref.shape[1]
    e = jnp.exp(scores_of(q_ref[...], prev_ref[:, :hd]))
    first = pos[0] == 0
    e = jnp.where(jnp.full(e.shape, first), 0.0, e)
    total = sum_ref[:, :1] + jnp.sum(e, axis=1, keepdims=True)
    inverse = 1.0 / total
    out = jnp.dot((e_ref[...] * inverse).astype(BF), kv_ref[:, hd:], preferred_element_type=F32)
    out += jnp.dot((e * inverse).astype(BF), prev_ref[:, hd:], preferred_element_type=F32)
    out_ref[...] = out.astype(BF)


def output_of(pos, pieces, w_own, w_other, core):
    a, _, b, y, _ = place(pos)
    hd = w_own.shape[1]
    total = None
    for i in range(4):
        yy = (y + i) & 3
        at = pl.multiple_of(((core + 2 * yy + 2 * y) & 7) * 2 * hd, 2 * hd)
        own = w_own[pl.ds(at, 2 * hd), :]
        other = w_other[pl.ds(at, 2 * hd), :]
        same = jnp.full(own.shape, a == b)
        rows = []
        for both in (jnp.where(same, own, other), jnp.where(same, other, own)):
            rows.append(jnp.concatenate([both[:hd], both[hd:]], axis=1))
        part = jnp.dot(pieces[i][...], jnp.concatenate(rows, axis=0), preferred_element_type=F32)
        total = part if total is None else total + part
    return total


def output_other_body(pos, *refs):
    pieces, (w_own, w_other, send_ref) = refs[:4], refs[4:]
    core = 1 - place(pos)[4]
    send_ref[...] = output_of(pos, pieces, w_own, w_other, core).astype(BF)


def output_own_body(pos, *refs):
    pieces, (w_own, w_other, hidden_ref, out_ref) = refs[:4], refs[4:]
    core = place(pos)[4]
    out_ref[...] = hidden_ref[...].astype(F32) + output_of(pos, pieces, w_own, w_other, core)


def add_body(own_ref, got_ref, out_ref):
    out_ref[...] = (own_ref[...] + got_ref[...].astype(F32)).astype(BF)


def swap_hi(a, z, b, y, k):
    return 1 - a, z, b, y, k


def swap_core(a, z, b, y, k):
    return a, z, b, y, 1 - k


def around(value):
    pieces = [value]
    for by in (1, 2, 3):
        pieces.append(permute(value, lambda a, z, b, y, k: (a, z, b, y - by, k)))
    return pieces


def layer(hidden, norm_gain, w_qkv, w_out):
    seg, feats = hidden.shape
    hd = w_out.shape[1]
    ctx, tp = lax.axis_index("ctx"), lax.axis_index("tp")
    pos = jnp.stack([ctx, tp]).astype(jnp.int32)
    same = (ctx >> 4) == (tp >> 3)

    piece = permute(w_out[0], lambda a, z, b, y, k: (b, z + 4 * y, a, z // 4, k))
    folded = (w_qkv[0].astype(F32) * norm_gain[0].astype(F32)[None, :, None]).astype(BF)
    chunk = jnp.concatenate([folded[0], folded[1], folded[2], piece], axis=1)
    parts = gather_z(chunk, tp & 1)

    corner = {(0, 0): (0, 1), (0, 1): (1, 1), (1, 1): (1, 0), (1, 0): (0, 0)}
    turn = permute(hidden, lambda a, z, b, y, k: (*_at(corner, a, b, z), y, k))
    cross = permute(hidden, lambda a, z, b, y, k: (b, z, a, y, k) if a != b else None)
    own = jnp.where(same, hidden, turn)
    other = jnp.where(same, turn, cross)
    blocks = []
    for block in around(jnp.concatenate([own, other], axis=0)):
        blocks += [block, permute(block, swap_core)]

    send, weights, out_w = call(
        project_other_body,
        (
            shape((seg, 4 * hd), BF),
            shape((16 * hd, 3 * hd), BF),
            shape((16 * hd, hd), BF),
        ),
        flops=2 * seg * 8 * feats * 3 * hd,
        nbytes=8 << 20,
    )(pos, *blocks, *parts)
    got = permute(send, swap_hi)
    own_part, own_ssq = call(
        project_own_body,
        (shape((seg, 3 * hd), F32), shape((seg, hd), F32)),
        flops=2 * seg * 8 * feats * 3 * hd,
        nbytes=8 << 20,
    )(pos, *blocks, weights)
    q, kv = call(
        lambda *refs: combine_body(*refs, features=16 * feats),
        (shape((seg, hd), BF), shape((seg, 2 * hd), BF)),
        nbytes=2 << 20,
        scalars=False,
    )(own_part, own_ssq, got)
    prev = lax.ppermute(kv, "ctx", [(i, i + 1) for i in range(31)])
    e_own, sum_own = call(
        own_body,
        (shape((seg, seg), F32), shape((seg, hd), F32)),
        flops=2 * seg * seg * hd,
        nbytes=2 << 20,
        scalars=False,
    )(q, kv)
    attended = call(
        attend_body, shape((seg, hd), BF), flops=6 * seg * seg * hd, nbytes=2 << 20
    )(pos, q, kv, prev, e_own, sum_own)

    facing = permute(attended, lambda a, z, b, y, k: (a, z, 1 - b, y, k))
    out_w_other = permute(out_w, swap_hi)
    pieces = around(jnp.concatenate([attended, facing], axis=1))
    sizes = dict(flops=2 * seg * feats * 8 * hd, nbytes=3 << 20)
    out_send = call(output_other_body, shape((seg, feats), BF), **sizes)(
        pos, *pieces, out_w, out_w_other
    )
    out_got = permute(out_send, swap_core)
    out_own = call(output_own_body, shape((seg, feats), F32), **sizes)(
        pos, *pieces, out_w, out_w_other, hidden
    )
    return call(add_body, shape((seg, feats), BF), scalars=False)(out_own, out_got)


def _at(corner, a, b, z):
    to = corner[a, b]
    return to[0], z, to[1]


def solution(mesh):
    placed = (P("ctx", "tp"), P(None, "ctx"), P(None, None, "ctx", "tp"), P(None, "tp", "ctx"))
    return jax.shard_map(
        layer, mesh=mesh, in_specs=placed, out_specs=P("ctx", "tp"), check_vma=False
    )
```

```python
import math

import jax
import jax.numpy as jnp
from jax import lax
from jax.experimental import pallas as pl
from jax.experimental.pallas import tpu as pltpu
from jax.sharding import PartitionSpec as P


INTERPRET = False
AXES = ("ctx", "tp")
BF = jnp.bfloat16
F32 = jnp.float32
STEPS = ((0, -4, 4, 8), (2, 6), (-2, -6), (1, -3, 5, 9), (-1, -5, 3, 7))


def pairs_of(target):
    pairs = []
    for src in range(512):
        ctx, tp = divmod(src, 16)
        a, z, b, y, k = ctx // 16, ctx % 16, tp // 8, tp // 2 % 4, tp % 2
        to = target(a, z, b, y, k)
        if to is not None:
            a, z, b, y, k = to
            pairs.append((src, (a * 16 + z % 16) * 16 + b * 8 + y % 4 * 2 + k))
    return pairs


def permute(value, target):
    return lax.ppermute(value, AXES, pairs_of(target))


def call(body, outs, scratch=(), flops=0, nbytes=1 << 20, vmem=24 << 20, scalars=True):
    def run(*args):
        specs = [pl.BlockSpec(memory_space=pltpu.VMEM) for _ in args]
        if scalars:
            specs[0] = pl.BlockSpec(memory_space=pltpu.SMEM)
        return pl.pallas_call(
            body,
            out_shape=outs,
            in_specs=specs,
            out_specs=jax.tree.map(lambda _: pl.BlockSpec(memory_space=pltpu.VMEM), outs),
            scratch_shapes=list(scratch),
            compiler_params=pltpu.CompilerParams(vmem_limit_bytes=vmem),
            cost_estimate=pl.CostEstimate(flops=flops, bytes_accessed=nbytes, transcendentals=0),
            interpret=INTERPRET,
        )(*args)

    return run


def shape(dims, dtype):
    return jax.ShapeDtypeStruct(dims, dtype)


def place(pos):
    ctx, tp = pos[0], pos[1]
    return ctx >> 4, ctx & 15, tp >> 3, (tp >> 1) & 3, tp & 1


def gather_z(chunk, core):
    def move(value, by):
        return permute(value, lambda a, z, b, y, k: (a, z + by, b, y, k))

    up4 = move(chunk, 4)
    down4 = move(chunk, -4)
    relay = permute(
        jnp.where(core == 0, down4, up4), lambda a, z, b, y, k: (a, z + (4 if k else 12), b, y, k)
    )
    down2 = move(jnp.concatenate([chunk, down4], axis=0), -2)
    up2 = move(jnp.concatenate([chunk, up4], axis=0), 2)
    held = jnp.concatenate([chunk, up4, down4, relay], axis=0)
    down1 = move(held, -1)
    up1 = move(held, 1)
    return held, down2, up2, down1, up1


def squares_body(*refs):
    blocks, (own_ref, other_ref) = refs[:8], refs[8:]
    seg = own_ref.shape[1]
    ones = jnp.ones((own_ref.shape[0], blocks[0].shape[1]), BF)
    for first, ref in ((0, own_ref), (seg, other_ref)):
        total = jnp.zeros(ref.shape, F32)
        for block in blocks:
            wider = block[first : first + seg, :].astype(F32)
            total += lax.dot_general(
                ones,
                (wider * wider).astype(BF),
                (((1,), (1,)), ((), ())),
                preferred_element_type=F32,
            )
        ref[...] = total


def project_rows(pos, blocks, weights, first, seg):
    _, _, _, y, k = place(pos)
    rows = weights.shape[0] // 16
    tile = min(seg, 256)
    for r in range(0, seg, tile):
        acc = jnp.zeros((tile, weights.shape[1]), F32)
        for i in range(8):
            yy = (y + i // 2) & 3
            kk = k if i % 2 == 0 else 1 - k
            at = pl.multiple_of((yy * 2 + kk) * 2 * rows, 2 * rows)
            block = blocks[i][first + r : first + r + tile, :]
            acc += jnp.dot(block, weights[pl.ds(at, 2 * rows), :], preferred_element_type=F32)
        yield slice(r, r + tile), acc


def project_other_body(pos, *refs):
    blocks, parts, (send_ref, w_ref, out_w_ref) = refs[:8], refs[8:13], refs[13:]
    _, z, _, _, _ = place(pos)
    rows = w_ref.shape[0] // 16
    seg, wide = send_ref.shape
    for part, steps in zip(parts, STEPS):
        for i, step in enumerate(steps):
            at = pl.multiple_of(((z + step + 16) & 15) * rows, rows)
            w_ref[pl.ds(at, rows), :] = part[i * rows : (i + 1) * rows, :wide]
            out_w_ref[pl.ds(at, rows), :] = part[i * rows : (i + 1) * rows, wide:]
    for at, acc in project_rows(pos, blocks, w_ref, seg, seg):
        send_ref[at, :] = acc.astype(BF)


def project_own_body(pos, *refs):
    blocks, (w_ref, own_ref) = refs[:8], refs[8:]
    for at, acc in project_rows(pos, blocks, w_ref, 0, own_ref.shape[0]):
        own_ref[at, :] = acc


def combine_body(own_ref, got_ref, ssq_ref, ssq_got_ref, q_ref, kv_ref, *, features):
    hd = q_ref.shape[1]
    scale = lax.rsqrt((ssq_ref[...] + ssq_got_ref[...]) * (1.0 / features) + 1e-06)
    column = lax.dot_general(
        scale,
        jnp.full((scale.shape[0], 3 * hd), 1.0 / scale.shape[0], F32),
        (((0,), (0,)), ((), ())),
        precision=lax.Precision.HIGHEST,
        preferred_element_type=F32,
    )
    total = (own_ref[...] + got_ref[...].astype(F32)) * column
    q_ref[...] = total[:, :hd].astype(BF)
    kv_ref[...] = total[:, hd:].astype(BF)


def scores_of(q, keys):
    hd = q.shape[1]
    return lax.dot_general(
        q, keys, (((1,), (1,)), ((), ())), preferred_element_type=F32
    ) * (1.0 / math.sqrt(hd))


def own_body(q_ref, kv_ref, e_ref, sum_ref):
    hd = q_ref.shape[1]
    scores = scores_of(q_ref[...], kv_ref[:, :hd])
    row = lax.broadcasted_iota(jnp.int32, scores.shape, 0)
    col = lax.broadcasted_iota(jnp.int32, scores.shape, 1)
    e = jnp.where(col <= row, jnp.exp(scores), 0.0)
    e_ref[...] = e
    sum_ref[...] = jnp.broadcast_to(jnp.sum(e, axis=1, keepdims=True), sum_ref.shape)


def attend_body(pos, q_ref, kv_ref, prev_ref, e_ref, sum_ref, out_ref):
    hd = q_ref.shape[1]
    e = jnp.exp(scores_of(q_ref[...], prev_ref[:, :hd]))
    first = pos[0] == 0
    e = jnp.where(jnp.full(e.shape, first), 0.0, e)
    total = sum_ref[:, :1] + jnp.sum(e, axis=1, keepdims=True)
    inverse = 1.0 / total
    out = jnp.dot((e_ref[...] * inverse).astype(BF), kv_ref[:, hd:], preferred_element_type=F32)
    out += jnp.dot((e * inverse).astype(BF), prev_ref[:, hd:], preferred_element_type=F32)
    out_ref[...] = out.astype(BF)


def output_of(pos, pieces, w_own, w_other, core):
    a, _, b, y, _ = place(pos)
    hd = w_own.shape[1]
    total = None
    for i in range(4):
        yy = (y + i) & 3
        at = pl.multiple_of(((core + 2 * yy + 2 * y) & 7) * 2 * hd, 2 * hd)
        own = w_own[pl.ds(at, 2 * hd), :]
        other = w_other[pl.ds(at, 2 * hd), :]
        same = jnp.full(own.shape, a == b)
        rows = []
        for both in (jnp.where(same, own, other), jnp.where(same, other, own)):
            rows.append(jnp.concatenate([both[:hd], both[hd:]], axis=1))
        part = jnp.dot(pieces[i][...], jnp.concatenate(rows, axis=0), preferred_element_type=F32)
        total = part if total is None else total + part
    return total


def output_other_body(pos, *refs):
    pieces, (w_own, w_other, send_ref) = refs[:4], refs[4:]
    core = 1 - place(pos)[4]
    send_ref[...] = output_of(pos, pieces, w_own, w_other, core).astype(BF)


def output_own_body(pos, *refs):
    pieces, (w_own, w_other, hidden_ref, out_ref) = refs[:4], refs[4:]
    core = place(pos)[4]
    out_ref[...] = hidden_ref[...].astype(F32) + output_of(pos, pieces, w_own, w_other, core)


def add_body(own_ref, got_ref, out_ref):
    out_ref[...] = (own_ref[...] + got_ref[...].astype(F32)).astype(BF)


def swap_hi(a, z, b, y, k):
    return 1 - a, z, b, y, k


def swap_core(a, z, b, y, k):
    return a, z, b, y, 1 - k


def around(value):
    pieces = [value]
    for by in (1, 2, 3):
        pieces.append(permute(value, lambda a, z, b, y, k: (a, z, b, y - by, k)))
    return pieces


def layer(hidden, norm_gain, w_qkv, w_out):
    seg, feats = hidden.shape
    hd = w_out.shape[1]
    ctx, tp = lax.axis_index("ctx"), lax.axis_index("tp")
    pos = jnp.stack([ctx, tp]).astype(jnp.int32)
    same = (ctx >> 4) == (tp >> 3)

    piece = permute(w_out[0], lambda a, z, b, y, k: (b, z + 4 * y, a, z // 4, k))
    folded = (w_qkv[0].astype(F32) * norm_gain[0].astype(F32)[None, :, None]).astype(BF)
    chunk = jnp.concatenate([folded[0], folded[1], folded[2], piece], axis=1)
    parts = gather_z(chunk, tp & 1)

    corner = {(0, 0): (0, 1), (0, 1): (1, 1), (1, 1): (1, 0), (1, 0): (0, 0)}
    turn = permute(hidden, lambda a, z, b, y, k: (*_at(corner, a, b, z), y, k))
    cross = permute(hidden, lambda a, z, b, y, k: (b, z, a, y, k) if a != b else None)
    own = jnp.where(same, hidden, turn)
    other = jnp.where(same, turn, cross)
    blocks = []
    for block in around(jnp.concatenate([own, other], axis=0)):
        blocks += [block, permute(block, swap_core)]

    ssq, ssq_send = call(
        squares_body,
        (shape((8, seg), F32), shape((8, seg), F32)),
        flops=4 * seg * 8 * feats * 8,
        nbytes=4 << 20,
        scalars=False,
    )(*blocks)
    ssq_got = permute(ssq_send, swap_hi)
    send, weights, out_w = call(
        project_other_body,
        (
            shape((seg, 3 * hd), BF),
            shape((16 * hd, 3 * hd), BF),
            shape((16 * hd, hd), BF),
        ),
        flops=2 * seg * 8 * feats * 3 * hd,
        nbytes=8 << 20,
    )(pos, *blocks, *parts)
    got = permute(send, swap_hi)
    own_part = call(
        project_own_body,
        shape((seg, 3 * hd), F32),
        flops=2 * seg * 8 * feats * 3 * hd,
        nbytes=8 << 20,
    )(pos, *blocks, weights)
    q, kv = call(
        lambda *refs: combine_body(*refs, features=16 * feats),
        (shape((seg, hd), BF), shape((seg, 2 * hd), BF)),
        nbytes=2 << 20,
        scalars=False,
    )(own_part, got, ssq, ssq_got)
    prev = lax.ppermute(kv, "ctx", [(i, i + 1) for i in range(31)])
    e_own, sum_own = call(
        own_body,
        (shape((seg, seg), F32), shape((seg, hd), F32)),
        flops=2 * seg * seg * hd,
        nbytes=2 << 20,
        scalars=False,
    )(q, kv)
    attended = call(
        attend_body, shape((seg, hd), BF), flops=6 * seg * seg * hd, nbytes=2 << 20
    )(pos, q, kv, prev, e_own, sum_own)

    facing = permute(attended, lambda a, z, b, y, k: (a, z, 1 - b, y, k))
    out_w_other = permute(out_w, swap_hi)
    pieces = around(jnp.concatenate([attended, facing], axis=1))
    sizes = dict(flops=2 * seg * feats * 8 * hd, nbytes=3 << 20)
    out_send = call(output_other_body, shape((seg, feats), BF), **sizes)(
        pos, *pieces, out_w, out_w_other
    )
    out_got = permute(out_send, swap_core)
    out_own = call(output_own_body, shape((seg, feats), F32), **sizes)(
        pos, *pieces, out_w, out_w_other, hidden
    )
    return call(add_body, shape((seg, feats), BF), scalars=False)(out_own, out_got)


def _at(corner, a, b, z):
    to = corner[a, b]
    return to[0], z, to[1]


def solution(mesh):
    placed = (P("ctx", "tp"), P(None, "ctx"), P(None, None, "ctx", "tp"), P(None, "tp", "ctx"))
    return jax.shard_map(
        layer, mesh=mesh, in_specs=placed, out_specs=P("ctx", "tp"), check_vma=False
    )
```

```python
import math

import jax
import jax.numpy as jnp
from jax import lax
from jax.experimental import pallas as pl
from jax.experimental.pallas import tpu as pltpu
from jax.sharding import PartitionSpec as P


INTERPRET = False
AXES = ("ctx", "tp")
BF = jnp.bfloat16
F32 = jnp.float32
REV = [int(f"{p:04b}"[::-1], 2) for p in range(16)]
STEPS = ((0, -4, 4, 8), (2, 6), (-2, -6), (1, -3, 5, 9), (-1, -5, 3, 7))


def pairs_of(target):
    pairs = []
    for src in range(512):
        ctx, tp = divmod(src, 16)
        a, z, b, y, k = ctx // 16, ctx % 16, tp // 8, tp // 2 % 4, tp % 2
        to = target(a, z, b, y, k)
        if to is not None:
            a, z, b, y, k = to
            pairs.append((src, (a * 16 + z % 16) * 16 + b * 8 + y % 4 * 2 + k))
    return pairs


def permute(value, target):
    return lax.ppermute(value, AXES, pairs_of(target))


def call(body, outs, scratch=(), flops=0, nbytes=1 << 20, vmem=24 << 20, scalars=True):
    def run(*args):
        specs = [pl.BlockSpec(memory_space=pltpu.VMEM) for _ in args]
        if scalars:
            specs[0] = pl.BlockSpec(memory_space=pltpu.SMEM)
        return pl.pallas_call(
            body,
            out_shape=outs,
            in_specs=specs,
            out_specs=jax.tree.map(lambda _: pl.BlockSpec(memory_space=pltpu.VMEM), outs),
            scratch_shapes=list(scratch),
            compiler_params=pltpu.CompilerParams(vmem_limit_bytes=vmem),
            cost_estimate=pl.CostEstimate(flops=flops, bytes_accessed=nbytes, transcendentals=0),
            interpret=INTERPRET,
        )(*args)

    return run


def shape(dims, dtype):
    return jax.ShapeDtypeStruct(dims, dtype)


def place(pos):
    ctx, tp = pos[0], pos[1]
    return ctx >> 4, ctx & 15, tp >> 3, (tp >> 1) & 3, tp & 1


def gather_z(chunk, core):
    def move(value, by):
        return permute(value, lambda a, z, b, y, k: (a, z + by, b, y, k))

    up4 = move(chunk, 4)
    down4 = move(chunk, -4)
    relay = permute(
        jnp.where(core == 0, down4, up4), lambda a, z, b, y, k: (a, z + (4 if k else 12), b, y, k)
    )
    down2 = move(jnp.concatenate([chunk, down4], axis=0), -2)
    up2 = move(jnp.concatenate([chunk, up4], axis=0), 2)
    held = jnp.concatenate([chunk, up4, down4, relay], axis=0)
    down1 = move(held, -1)
    up1 = move(held, 1)
    return held, down2, up2, down1, up1


def squares_body(*refs):
    blocks, (own_ref, other_ref) = refs[:8], refs[8:]
    seg = own_ref.shape[1]
    ones = jnp.ones((own_ref.shape[0], blocks[0].shape[1]), BF)
    for first, ref in ((0, own_ref), (seg, other_ref)):
        total = jnp.zeros(ref.shape, F32)
        for block in blocks:
            wider = block[first : first + seg, :].astype(F32)
            total += lax.dot_general(
                ones,
                (wider * wider).astype(BF),
                (((1,), (1,)), ((), ())),
                preferred_element_type=F32,
            )
        ref[...] = total


def double_z(chunk):
    held = chunk
    for by in (8, 4, 2, 1):
        got = permute(held, lambda a, z, b, y, k: (a, z + (16 - by if k else by), b, y, k))
        if by > 1:
            held = jnp.concatenate([held, got], axis=0)
    return held, got


def project_rows(pos, blocks, weights, first, seg):
    _, _, _, y, k = place(pos)
    rows = weights.shape[0] // 16
    tile = min(seg, 256)
    for r in range(0, seg, tile):
        acc = jnp.zeros((tile, weights.shape[1]), F32)
        for i in range(8):
            yy = (y + i // 2) & 3
            kk = k if i % 2 == 0 else 1 - k
            at = pl.multiple_of((yy * 2 + kk) * 2 * rows, 2 * rows)
            block = blocks[i][first + r : first + r + tile, :]
            acc += jnp.dot(block, weights[pl.ds(at, 2 * rows), :], preferred_element_type=F32)
        yield slice(r, r + tile), acc


def project_other_body(pos, *refs):
    blocks, parts, (kv_ref, q_ref, w_ref) = refs[:8], refs[8:13], refs[13:]
    _, z, _, _, _ = place(pos)
    rows = w_ref.shape[0] // 16
    seg, hd = q_ref.shape
    for part, steps in zip(parts, STEPS):
        for i, step in enumerate(steps):
            at = pl.multiple_of(((z + step + 16) & 15) * rows, rows)
            w_ref[pl.ds(at, rows), :] = part[i * rows : (i + 1) * rows, :]
    for at, acc in project_rows(pos, blocks, w_ref, seg, seg):
        q_ref[at, :] = acc[:, :hd].astype(BF)
        kv_ref[at, :] = acc[:, hd:].astype(BF)


def project_own_body(pos, *refs):
    blocks, (w_ref, own_ref) = refs[:8], refs[8:]
    for at, acc in project_rows(pos, blocks, w_ref, 0, own_ref.shape[0]):
        own_ref[at, :] = acc


def combine_body(own_ref, got_ref, ssq_ref, ssq_got_ref, out_ref, *, features, first):
    wide = out_ref.shape[1]
    scale = lax.rsqrt((ssq_ref[...] + ssq_got_ref[...]) * (1.0 / features) + 1e-06)
    column = lax.dot_general(
        scale,
        jnp.full((scale.shape[0], wide), 1.0 / scale.shape[0], F32),
        (((0,), (0,)), ((), ())),
        precision=lax.Precision.HIGHEST,
        preferred_element_type=F32,
    )
    own = own_ref[:, first : first + wide]
    out_ref[...] = ((own + got_ref[...].astype(F32)) * column).astype(BF)


def scores_of(q, keys):
    hd = q.shape[1]
    return lax.dot_general(
        q, keys, (((1,), (1,)), ((), ())), preferred_element_type=F32
    ) * (1.0 / math.sqrt(hd))


def own_body(q_ref, kv_ref, e_ref, sum_ref):
    hd = q_ref.shape[1]
    scores = scores_of(q_ref[...], kv_ref[:, :hd])
    row = lax.broadcasted_iota(jnp.int32, scores.shape, 0)
    col = lax.broadcasted_iota(jnp.int32, scores.shape, 1)
    e = jnp.where(col <= row, jnp.exp(scores), 0.0)
    e_ref[...] = e
    sum_ref[...] = jnp.broadcast_to(jnp.sum(e, axis=1, keepdims=True), sum_ref.shape)


def attend_body(pos, q_ref, kv_ref, prev_ref, e_ref, sum_ref, out_ref):
    hd = q_ref.shape[1]
    e = jnp.exp(scores_of(q_ref[...], prev_ref[:, :hd]))
    first = pos[0] == 0
    e = jnp.where(jnp.full(e.shape, first), 0.0, e)
    total = sum_ref[:, :1] + jnp.sum(e, axis=1, keepdims=True)
    inverse = 1.0 / total
    out = jnp.dot((e_ref[...] * inverse).astype(BF), kv_ref[:, hd:], preferred_element_type=F32)
    out += jnp.dot((e * inverse).astype(BF), prev_ref[:, hd:], preferred_element_type=F32)
    out_ref[...] = out.astype(BF)


def output_of(pos, pieces, w_ref, core):
    a, _, b, y, _ = place(pos)
    hd = w_ref.shape[1] // 2
    total = None
    for i in range(4):
        yy = (y + i) & 3
        at = pl.multiple_of(((core + 2 * yy + 2 * y) & 7) * 2 * hd, 2 * hd)
        both = w_ref[pl.ds(at, 2 * hd), :]
        own, other = both[:, :hd], both[:, hd:]
        same = jnp.full(own.shape, a == b)
        rows = []
        for half in (jnp.where(same, own, other), jnp.where(same, other, own)):
            rows.append(jnp.concatenate([half[:hd], half[hd:]], axis=1))
        part = jnp.dot(pieces[i][...], jnp.concatenate(rows, axis=0), preferred_element_type=F32)
        total = part if total is None else total + part
    return total


def output_other_body(pos, *refs):
    pieces, (w_lo, w_hi, send_ref, w_ref) = refs[:4], refs[4:]
    _, z, _, _, k = place(pos)
    rows = w_ref.shape[0] // 16
    for p in range(16):
        at = pl.multiple_of(((z - (1 - 2 * k) * REV[p] + 16) & 15) * rows, rows)
        half = w_lo if p < 8 else w_hi
        w_ref[pl.ds(at, rows), :] = half[p % 8 * rows : (p % 8 + 1) * rows, :]
    send_ref[...] = output_of(pos, pieces, w_ref, 1 - k).astype(BF)


def output_own_body(pos, *refs):
    pieces, (w_ref, hidden_ref, out_ref) = refs[:4], refs[4:]
    core = place(pos)[4]
    out_ref[...] = hidden_ref[...].astype(F32) + output_of(pos, pieces, w_ref, core)


def add_body(own_ref, got_ref, out_ref):
    out_ref[...] = (own_ref[...] + got_ref[...].astype(F32)).astype(BF)


def swap_hi(a, z, b, y, k):
    return 1 - a, z, b, y, k


def swap_core(a, z, b, y, k):
    return a, z, b, y, 1 - k


def around(value):
    pieces = [value]
    for by in (1, 2, 3):
        pieces.append(permute(value, lambda a, z, b, y, k: (a, z, b, y - by, k)))
    return pieces


def layer(hidden, norm_gain, w_qkv, w_out):
    seg, feats = hidden.shape
    hd = w_out.shape[1]
    ctx, tp = lax.axis_index("ctx"), lax.axis_index("tp")
    pos = jnp.stack([ctx, tp]).astype(jnp.int32)
    same = (ctx >> 4) == (tp >> 3)

    folded = (w_qkv[0].astype(F32) * norm_gain[0].astype(F32)[None, :, None]).astype(BF)
    chunk = jnp.concatenate([folded[0], folded[1], folded[2]], axis=1)
    parts = gather_z(chunk, tp & 1)

    corner = {(0, 0): (0, 1), (0, 1): (1, 1), (1, 1): (1, 0), (1, 0): (0, 0)}
    turn = permute(hidden, lambda a, z, b, y, k: (*_at(corner, a, b, z), y, k))
    cross = permute(hidden, lambda a, z, b, y, k: (b, z, a, y, k) if a != b else None)
    own = jnp.where(same, hidden, turn)
    other = jnp.where(same, turn, cross)
    blocks = []
    for block in around(jnp.concatenate([own, other], axis=0)):
        blocks += [block, permute(block, swap_core)]

    piece_a = permute(w_out[0], lambda a, z, b, y, k: (b, z + 4 * y, a, z // 4, k))
    piece_b = permute(w_out[0], lambda a, z, b, y, k: (1 - b, z + 4 * y, a, z // 4, k))
    o_lo, o_hi = double_z(jnp.concatenate([piece_a, piece_b], axis=1))

    ssq, ssq_send = call(
        squares_body,
        (shape((8, seg), F32), shape((8, seg), F32)),
        flops=4 * seg * 8 * feats * 8,
        nbytes=4 << 20,
        scalars=False,
    )(*blocks)
    ssq_got = permute(ssq_send, swap_hi)
    kv_send, q_send, weights = call(
        project_other_body,
        (shape((seg, 2 * hd), BF), shape((seg, hd), BF), shape((16 * hd, 3 * hd), BF)),
        flops=2 * seg * 8 * feats * 3 * hd,
        nbytes=8 << 20,
    )(pos, *blocks, *parts)
    kv_got = permute(kv_send, swap_hi)
    q_got = permute(q_send, swap_hi)
    own_part = call(
        project_own_body,
        shape((seg, 3 * hd), F32),
        flops=2 * seg * 8 * feats * 3 * hd,
        nbytes=8 << 20,
    )(pos, *blocks, weights)

    def combine(got, first):
        return call(
            lambda *refs: combine_body(*refs, features=16 * feats, first=first),
            shape(got.shape, BF),
            nbytes=1 << 20,
            scalars=False,
        )(own_part, got, ssq, ssq_got)

    kv = combine(kv_got, hd)
    q = combine(q_got, 0)
    prev = lax.ppermute(kv, "ctx", [(i, i + 1) for i in range(31)])
    e_own, sum_own = call(
        own_body,
        (shape((seg, seg), F32), shape((seg, hd), F32)),
        flops=2 * seg * seg * hd,
        nbytes=2 << 20,
        scalars=False,
    )(q, kv)
    attended = call(
        attend_body, shape((seg, hd), BF), flops=6 * seg * seg * hd, nbytes=2 << 20
    )(pos, q, kv, prev, e_own, sum_own)

    facing = permute(attended, lambda a, z, b, y, k: (a, z, 1 - b, y, k))
    pieces = around(jnp.concatenate([attended, facing], axis=1))
    sizes = dict(flops=2 * seg * feats * 8 * hd, nbytes=3 << 20)
    out_send, out_w = call(
        output_other_body, (shape((seg, feats), BF), shape((16 * hd, 2 * hd), BF)), **sizes
    )(pos, *pieces, o_lo, o_hi)
    out_got = permute(out_send, swap_core)
    out_own = call(output_own_body, shape((seg, feats), F32), **sizes)(
        pos, *pieces, out_w, hidden
    )
    return call(add_body, shape((seg, feats), BF), scalars=False)(out_own, out_got)


def _at(corner, a, b, z):
    to = corner[a, b]
    return to[0], z, to[1]


def solution(mesh):
    placed = (P("ctx", "tp"), P(None, "ctx"), P(None, None, "ctx", "tp"), P(None, "tp", "ctx"))
    return jax.shard_map(
        layer, mesh=mesh, in_specs=placed, out_specs=P("ctx", "tp"), check_vma=False
    )
```

```python
import math

import jax
import jax.numpy as jnp
from jax import lax
from jax.experimental import pallas as pl
from jax.experimental.pallas import tpu as pltpu
from jax.sharding import PartitionSpec as P


INTERPRET = False
AXES = ("ctx", "tp")
BF = jnp.bfloat16
F32 = jnp.float32
HELD = (0, -4, 4, 8)


def pairs_of(target):
    pairs = []
    for src in range(512):
        ctx, tp = divmod(src, 16)
        a, z, b, y, k = ctx // 16, ctx % 16, tp // 8, tp // 2 % 4, tp % 2
        to = target(a, z, b, y, k)
        if to is not None:
            a, z, b, y, k = to
            pairs.append((src, (a * 16 + z % 16) * 16 + b * 8 + y % 4 * 2 + k))
    return pairs


def permute(value, target):
    return lax.ppermute(value, AXES, pairs_of(target))


def call(body, outs, scratch=(), flops=0, nbytes=1 << 20, vmem=24 << 20, scalars=True):
    def run(*args):
        specs = [pl.BlockSpec(memory_space=pltpu.VMEM) for _ in args]
        if scalars:
            specs[0] = pl.BlockSpec(memory_space=pltpu.SMEM)
        return pl.pallas_call(
            body,
            out_shape=outs,
            in_specs=specs,
            out_specs=jax.tree.map(lambda _: pl.BlockSpec(memory_space=pltpu.VMEM), outs),
            scratch_shapes=list(scratch),
            compiler_params=pltpu.CompilerParams(vmem_limit_bytes=vmem),
            cost_estimate=pl.CostEstimate(flops=flops, bytes_accessed=nbytes, transcendentals=0),
            interpret=INTERPRET,
        )(*args)

    return run


def shape(dims, dtype):
    return jax.ShapeDtypeStruct(dims, dtype)


def place(pos):
    ctx, tp = pos[0], pos[1]
    return ctx >> 4, ctx & 15, tp >> 3, (tp >> 1) & 3, tp & 1


def gather_z(chunk, core):
    def move(value, by):
        return permute(value, lambda a, z, b, y, k: (a, z + by, b, y, k))

    up4 = move(chunk, 4)
    down4 = move(chunk, -4)
    relay = permute(
        jnp.where(core == 0, down4, up4), lambda a, z, b, y, k: (a, z + (4 if k else 12), b, y, k)
    )
    held = jnp.concatenate([chunk, up4, down4, relay], axis=0)
    two = permute(held, lambda a, z, b, y, k: (a, z + (2 if k else 14), b, y, k))
    return held, two, move(held, -1), move(held, 1)


def columns_of(blocks, i, first, size):
    if i % 2 == 0:
        return blocks[i // 2][first : first + size, :]
    first += i // 2 * blocks[0].shape[0]
    return blocks[4][first : first + size, :]


def squares_body(*refs):
    blocks, (own_ref, other_ref) = refs[:5], refs[5:]
    seg = own_ref.shape[1]
    ones = jnp.ones((own_ref.shape[0], blocks[0].shape[1]), BF)
    for first, ref in ((0, own_ref), (seg, other_ref)):
        total = jnp.zeros(ref.shape, F32)
        for i in range(8):
            wider = columns_of(blocks, i, first, seg).astype(F32)
            total += lax.dot_general(
                ones,
                (wider * wider).astype(BF),
                (((1,), (1,)), ((), ())),
                preferred_element_type=F32,
            )
        ref[...] = total


def project_rows(pos, blocks, weights, first, seg):
    _, _, _, y, k = place(pos)
    rows = weights.shape[0] // 16
    tile = min(seg, 256)
    for r in range(0, seg, tile):
        acc = jnp.zeros((tile, weights.shape[1]), F32)
        for i in range(8):
            yy = (y + i // 2) & 3
            kk = k if i % 2 == 0 else 1 - k
            at = pl.multiple_of((yy * 2 + kk) * 2 * rows, 2 * rows)
            block = columns_of(blocks, i, first + r, tile)
            acc += jnp.dot(block, weights[pl.ds(at, 2 * rows), :], preferred_element_type=F32)
        yield slice(r, r + tile), acc


def project_other_body(pos, *refs):
    blocks, parts, (kv_ref, q_ref, w_ref, out_w_ref) = refs[:5], refs[5:9], refs[9:]
    _, z, _, _, k = place(pos)
    rows = w_ref.shape[0] // 16
    seg, hd = q_ref.shape
    wide = w_ref.shape[1]
    for part, base in zip(parts, (0, 2 - 4 * k, 1, -1)):
        for i, step in enumerate(HELD):
            at = pl.multiple_of(((z + base + step + 16) & 15) * rows, rows)
            w_ref[pl.ds(at, rows), :] = part[i * rows : (i + 1) * rows, :wide]
            out_w_ref[pl.ds(at, rows), :] = part[i * rows : (i + 1) * rows, wide:]
    for at, acc in project_rows(pos, blocks, w_ref, seg, seg):
        q_ref[at, :] = acc[:, :hd].astype(BF)
        kv_ref[at, :] = acc[:, hd:].astype(BF)


def project_own_body(pos, *refs):
    blocks, (w_ref, own_ref) = refs[:5], refs[5:]
    for at, acc in project_rows(pos, blocks, w_ref, 0, own_ref.shape[0]):
        own_ref[at, :] = acc


def combine_body(own_ref, got_ref, ssq_ref, ssq_got_ref, out_ref, *, features, first):
    wide = out_ref.shape[1]
    scale = lax.rsqrt((ssq_ref[...] + ssq_got_ref[...]) * (1.0 / features) + 1e-06)
    column = lax.dot_general(
        scale,
        jnp.full((scale.shape[0], wide), 1.0 / scale.shape[0], F32),
        (((0,), (0,)), ((), ())),
        precision=lax.Precision.HIGHEST,
        preferred_element_type=F32,
    )
    own = own_ref[:, first : first + wide]
    out_ref[...] = ((own + got_ref[...].astype(F32)) * column).astype(BF)


def scores_of(q, keys):
    hd = q.shape[1]
    return lax.dot_general(
        q, keys, (((1,), (1,)), ((), ())), preferred_element_type=F32
    ) * (1.0 / math.sqrt(hd))


def own_body(q_ref, kv_ref, e_ref, sum_ref):
    hd = q_ref.shape[1]
    scores = scores_of(q_ref[...], kv_ref[:, :hd])
    row = lax.broadcasted_iota(jnp.int32, scores.shape, 0)
    col = lax.broadcasted_iota(jnp.int32, scores.shape, 1)
    e = jnp.where(col <= row, jnp.exp(scores), 0.0)
    e_ref[...] = e
    sum_ref[...] = jnp.broadcast_to(jnp.sum(e, axis=1, keepdims=True), sum_ref.shape)


def attend_body(pos, q_ref, kv_ref, prev_ref, e_ref, sum_ref, out_ref):
    hd = q_ref.shape[1]
    e = jnp.exp(scores_of(q_ref[...], prev_ref[:, :hd]))
    first = pos[0] == 0
    e = jnp.where(jnp.full(e.shape, first), 0.0, e)
    total = sum_ref[:, :1] + jnp.sum(e, axis=1, keepdims=True)
    inverse = 1.0 / total
    out = jnp.dot((e_ref[...] * inverse).astype(BF), kv_ref[:, hd:], preferred_element_type=F32)
    out += jnp.dot((e * inverse).astype(BF), prev_ref[:, hd:], preferred_element_type=F32)
    out_ref[...] = out.astype(BF)


def output_of(pos, pieces, w_own, w_other, core):
    a, _, b, y, _ = place(pos)
    hd = w_own.shape[1]
    total = None
    for i in range(4):
        yy = (y + i) & 3
        at = pl.multiple_of(((core + 2 * yy + 2 * y) & 7) * 2 * hd, 2 * hd)
        own = w_own[pl.ds(at, 2 * hd), :]
        other = w_other[pl.ds(at, 2 * hd), :]
        same = jnp.full(own.shape, a == b)
        rows = []
        for both in (jnp.where(same, own, other), jnp.where(same, other, own)):
            rows.append(jnp.concatenate([both[:hd], both[hd:]], axis=1))
        part = jnp.dot(pieces[i][...], jnp.concatenate(rows, axis=0), preferred_element_type=F32)
        total = part if total is None else total + part
    return total


def output_other_body(pos, *refs):
    pieces, (w_own, w_other, send_ref) = refs[:4], refs[4:]
    core = 1 - place(pos)[4]
    send_ref[...] = output_of(pos, pieces, w_own, w_other, core).astype(BF)


def output_own_body(pos, *refs):
    pieces, (w_own, w_other, hidden_ref, out_ref) = refs[:4], refs[4:]
    core = place(pos)[4]
    out_ref[...] = hidden_ref[...].astype(F32) + output_of(pos, pieces, w_own, w_other, core)


def add_body(own_ref, got_ref, out_ref):
    out_ref[...] = (own_ref[...] + got_ref[...].astype(F32)).astype(BF)


def swap_hi(a, z, b, y, k):
    return 1 - a, z, b, y, k


def swap_core(a, z, b, y, k):
    return a, z, b, y, 1 - k


def around(value):
    pieces = [value]
    for by in (1, 2, 3):
        pieces.append(permute(value, lambda a, z, b, y, k: (a, z, b, y - by, k)))
    return pieces


def layer(hidden, norm_gain, w_qkv, w_out):
    seg, feats = hidden.shape
    hd = w_out.shape[1]
    ctx, tp = lax.axis_index("ctx"), lax.axis_index("tp")
    pos = jnp.stack([ctx, tp]).astype(jnp.int32)
    same = (ctx >> 4) == (tp >> 3)

    piece = permute(w_out[0], lambda a, z, b, y, k: (b, z + 4 * y, a, z // 4, k))
    folded = (w_qkv[0].astype(F32) * norm_gain[0].astype(F32)[None, :, None]).astype(BF)
    chunk = jnp.concatenate([folded[0], folded[1], folded[2], piece], axis=1)
    parts = gather_z(chunk, tp & 1)

    corner = {(0, 0): (0, 1), (0, 1): (1, 1), (1, 1): (1, 0), (1, 0): (0, 0)}
    turn = permute(hidden, lambda a, z, b, y, k: (*_at(corner, a, b, z), y, k))
    cross = permute(hidden, lambda a, z, b, y, k: (b, z, a, y, k) if a != b else None)
    own = jnp.where(same, hidden, turn)
    other = jnp.where(same, turn, cross)
    blocks = around(jnp.concatenate([own, other], axis=0))
    blocks.append(permute(jnp.concatenate(blocks, axis=0), swap_core))

    ssq, ssq_send = call(
        squares_body,
        (shape((8, seg), F32), shape((8, seg), F32)),
        flops=4 * seg * 8 * feats * 8,
        nbytes=4 << 20,
        scalars=False,
    )(*blocks)
    ssq_got = permute(ssq_send, swap_hi)
    kv_send, q_send, weights, out_w = call(
        project_other_body,
        (
            shape((seg, 2 * hd), BF),
            shape((seg, hd), BF),
            shape((16 * hd, 3 * hd), BF),
            shape((16 * hd, hd), BF),
        ),
        flops=2 * seg * 8 * feats * 3 * hd,
        nbytes=8 << 20,
    )(pos, *blocks, *parts)
    kv_got = permute(kv_send, swap_hi)
    q_got = permute(q_send, swap_hi)
    own_part = call(
        project_own_body,
        shape((seg, 3 * hd), F32),
        flops=2 * seg * 8 * feats * 3 * hd,
        nbytes=8 << 20,
    )(pos, *blocks, weights)

    def combine(got, first):
        return call(
            lambda *refs: combine_body(*refs, features=16 * feats, first=first),
            shape(got.shape, BF),
            nbytes=1 << 20,
            scalars=False,
        )(own_part, got, ssq, ssq_got)

    kv = combine(kv_got, hd)
    q = combine(q_got, 0)
    prev = lax.ppermute(kv, "ctx", [(i, i + 1) for i in range(31)])
    e_own, sum_own = call(
        own_body,
        (shape((seg, seg), F32), shape((seg, hd), F32)),
        flops=2 * seg * seg * hd,
        nbytes=2 << 20,
        scalars=False,
    )(q, kv)
    attended = call(
        attend_body, shape((seg, hd), BF), flops=6 * seg * seg * hd, nbytes=2 << 20
    )(pos, q, kv, prev, e_own, sum_own)

    facing = permute(attended, lambda a, z, b, y, k: (a, z, 1 - b, y, k))
    out_w_other = permute(out_w, swap_hi)
    pieces = around(jnp.concatenate([attended, facing], axis=1))
    sizes = dict(flops=2 * seg * feats * 8 * hd, nbytes=3 << 20)
    out_send = call(output_other_body, shape((seg, feats), BF), **sizes)(
        pos, *pieces, out_w, out_w_other
    )
    out_got = permute(out_send, swap_core)
    out_own = call(output_own_body, shape((seg, feats), F32), **sizes)(
        pos, *pieces, out_w, out_w_other, hidden
    )
    return call(add_body, shape((seg, feats), BF), scalars=False)(out_own, out_got)


def _at(corner, a, b, z):
    to = corner[a, b]
    return to[0], z, to[1]


def solution(mesh):
    placed = (P("ctx", "tp"), P(None, "ctx"), P(None, None, "ctx", "tp"), P(None, "tp", "ctx"))
    return jax.shard_map(
        layer, mesh=mesh, in_specs=placed, out_specs=P("ctx", "tp"), check_vma=False
    )
```

```python
import math

import jax
import jax.numpy as jnp
from jax import lax
from jax.experimental import pallas as pl
from jax.experimental.pallas import tpu as pltpu
from jax.sharding import PartitionSpec as P


INTERPRET = False
AXES = ("ctx", "tp")
BF = jnp.bfloat16
F32 = jnp.float32
STEPS = ((0, -4, 4, 8), (2, 6), (-2, -6), (1, -3, 5, 9), (-1, -5, 3, 7))


def pairs_of(target):
    pairs = []
    for src in range(512):
        ctx, tp = divmod(src, 16)
        a, z, b, y, k = ctx // 16, ctx % 16, tp // 8, tp // 2 % 4, tp % 2
        to = target(a, z, b, y, k)
        if to is not None:
            a, z, b, y, k = to
            pairs.append((src, (a * 16 + z % 16) * 16 + b * 8 + y % 4 * 2 + k))
    return pairs


def permute(value, target):
    return lax.ppermute(value, AXES, pairs_of(target))


def call(body, outs, scratch=(), flops=0, nbytes=1 << 20, vmem=24 << 20, scalars=True):
    def run(*args):
        specs = [pl.BlockSpec(memory_space=pltpu.VMEM) for _ in args]
        if scalars:
            specs[0] = pl.BlockSpec(memory_space=pltpu.SMEM)
        return pl.pallas_call(
            body,
            out_shape=outs,
            in_specs=specs,
            out_specs=jax.tree.map(lambda _: pl.BlockSpec(memory_space=pltpu.VMEM), outs),
            scratch_shapes=list(scratch),
            compiler_params=pltpu.CompilerParams(vmem_limit_bytes=vmem),
            cost_estimate=pl.CostEstimate(flops=flops, bytes_accessed=nbytes, transcendentals=0),
            interpret=INTERPRET,
        )(*args)

    return run


def shape(dims, dtype):
    return jax.ShapeDtypeStruct(dims, dtype)


def place(pos):
    ctx, tp = pos[0], pos[1]
    return ctx >> 4, ctx & 15, tp >> 3, (tp >> 1) & 3, tp & 1


def gather_z(chunk, core):
    def move(value, by):
        return permute(value, lambda a, z, b, y, k: (a, z + by, b, y, k))

    up4 = move(chunk, 4)
    down4 = move(chunk, -4)
    relay = permute(
        jnp.where(core == 0, down4, up4), lambda a, z, b, y, k: (a, z + (4 if k else 12), b, y, k)
    )
    down2 = move(jnp.concatenate([chunk, down4], axis=0), -2)
    up2 = move(jnp.concatenate([chunk, up4], axis=0), 2)
    held = jnp.concatenate([chunk, up4, down4, relay], axis=0)
    down1 = move(held, -1)
    up1 = move(held, 1)
    return held, down2, up2, down1, up1


def squares_body(*refs):
    blocks, (own_ref, other_ref) = refs[:8], refs[8:]
    seg = own_ref.shape[1]
    ones = jnp.ones((own_ref.shape[0], blocks[0].shape[1]), BF)
    for first, ref in ((0, own_ref), (seg, other_ref)):
        total = jnp.zeros(ref.shape, F32)
        for block in blocks:
            wider = block[first : first + seg, :].astype(F32)
            total += lax.dot_general(
                ones,
                (wider * wider).astype(BF),
                (((1,), (1,)), ((), ())),
                preferred_element_type=F32,
            )
        ref[...] = total


def project_rows(pos, blocks, weights, first, seg):
    _, _, _, y, k = place(pos)
    rows = weights.shape[0] // 16
    tile = min(seg, 256)
    for r in range(0, seg, tile):
        acc = jnp.zeros((tile, weights.shape[1]), F32)
        for i in range(8):
            yy = (y + i // 2) & 3
            kk = k if i % 2 == 0 else 1 - k
            at = pl.multiple_of((yy * 2 + kk) * 2 * rows, 2 * rows)
            block = blocks[i][first + r : first + r + tile, :]
            acc += jnp.dot(block, weights[pl.ds(at, 2 * rows), :], preferred_element_type=F32)
        yield slice(r, r + tile), acc


def project_other_body(pos, *refs):
    blocks, parts, (kv_ref, q_ref, w_ref, out_w_ref) = refs[:8], refs[8:13], refs[13:]
    _, z, _, _, _ = place(pos)
    rows = w_ref.shape[0] // 16
    seg, hd = q_ref.shape
    wide = w_ref.shape[1]
    for part, steps in zip(parts, STEPS):
        for i, step in enumerate(steps):
            at = pl.multiple_of(((z + step + 16) & 15) * rows, rows)
            w_ref[pl.ds(at, rows), :] = part[i * rows : (i + 1) * rows, :wide]
            out_w_ref[pl.ds(at, rows), :] = part[i * rows : (i + 1) * rows, wide:]
    for at, acc in project_rows(pos, blocks, w_ref, seg, seg):
        q_ref[at, :] = acc[:, :hd].astype(BF)
        kv_ref[at, :] = acc[:, hd:].astype(BF)


def project_own_body(pos, *refs):
    blocks, (w_ref, own_ref) = refs[:8], refs[8:]
    for at, acc in project_rows(pos, blocks, w_ref, 0, own_ref.shape[0]):
        own_ref[at, :] = acc


def combine_body(own_ref, got_ref, ssq_ref, ssq_got_ref, out_ref, *, features, first):
    wide = out_ref.shape[1]
    scale = lax.rsqrt((ssq_ref[...] + ssq_got_ref[...]) * (1.0 / features) + 1e-06)
    column = lax.dot_general(
        scale,
        jnp.full((scale.shape[0], wide), 1.0 / scale.shape[0], F32),
        (((0,), (0,)), ((), ())),
        precision=lax.Precision.HIGHEST,
        preferred_element_type=F32,
    )
    own = own_ref[:, first : first + wide]
    out_ref[...] = ((own + got_ref[...].astype(F32)) * column).astype(BF)


def scores_of(q, keys):
    hd = q.shape[1]
    return lax.dot_general(
        q, keys, (((1,), (1,)), ((), ())), preferred_element_type=F32
    ) * (1.0 / math.sqrt(hd))


def own_body(q_ref, kv_ref, e_ref, sum_ref):
    hd = q_ref.shape[1]
    scores = scores_of(q_ref[...], kv_ref[:, :hd])
    row = lax.broadcasted_iota(jnp.int32, scores.shape, 0)
    col = lax.broadcasted_iota(jnp.int32, scores.shape, 1)
    e = jnp.where(col <= row, jnp.exp(scores), 0.0)
    e_ref[...] = e
    sum_ref[...] = jnp.broadcast_to(jnp.sum(e, axis=1, keepdims=True), sum_ref.shape)


def attend_body(pos, q_ref, kv_ref, prev_ref, e_ref, sum_ref, out_ref):
    hd = q_ref.shape[1]
    e = jnp.exp(scores_of(q_ref[...], prev_ref[:, :hd]))
    first = pos[0] == 0
    e = jnp.where(jnp.full(e.shape, first), 0.0, e)
    total = sum_ref[:, :1] + jnp.sum(e, axis=1, keepdims=True)
    inverse = 1.0 / total
    out = jnp.dot((e_ref[...] * inverse).astype(BF), kv_ref[:, hd:], preferred_element_type=F32)
    out += jnp.dot((e * inverse).astype(BF), prev_ref[:, hd:], preferred_element_type=F32)
    out_ref[...] = out.astype(BF)


def output_of(pos, pieces, w_own, w_other, core):
    a, _, b, y, _ = place(pos)
    hd = w_own.shape[1]
    total = None
    for i in range(4):
        yy = (y + i) & 3
        at = pl.multiple_of(((core + 2 * yy + 2 * y) & 7) * 2 * hd, 2 * hd)
        own = w_own[pl.ds(at, 2 * hd), :]
        other = w_other[pl.ds(at, 2 * hd), :]
        same = jnp.full(own.shape, a == b)
        rows = []
        for both in (jnp.where(same, own, other), jnp.where(same, other, own)):
            rows.append(jnp.concatenate([both[:hd], both[hd:]], axis=1))
        part = jnp.dot(pieces[i][...], jnp.concatenate(rows, axis=0), preferred_element_type=F32)
        total = part if total is None else total + part
    return total


def output_other_body(pos, *refs):
    pieces, (w_own, w_other, send_ref) = refs[:4], refs[4:]
    core = 1 - place(pos)[4]
    send_ref[...] = output_of(pos, pieces, w_own, w_other, core).astype(BF)


def output_own_body(pos, *refs):
    pieces, (w_own, w_other, hidden_ref, out_ref) = refs[:4], refs[4:]
    core = place(pos)[4]
    out_ref[...] = hidden_ref[...].astype(F32) + output_of(pos, pieces, w_own, w_other, core)


def add_body(own_ref, got_ref, out_ref):
    out_ref[...] = (own_ref[...] + got_ref[...].astype(F32)).astype(BF)


def swap_hi(a, z, b, y, k):
    return 1 - a, z, b, y, k


def swap_core(a, z, b, y, k):
    return a, z, b, y, 1 - k


def around(value):
    pieces = [value]
    for by in (1, 2, 3):
        pieces.append(permute(value, lambda a, z, b, y, k: (a, z, b, y - by, k)))
    return pieces


def layer(hidden, norm_gain, w_qkv, w_out):
    seg, feats = hidden.shape
    hd = w_out.shape[1]
    ctx, tp = lax.axis_index("ctx"), lax.axis_index("tp")
    pos = jnp.stack([ctx, tp]).astype(jnp.int32)
    same = (ctx >> 4) == (tp >> 3)

    piece = permute(w_out[0], lambda a, z, b, y, k: (b, z + 4 * y, a, z // 4, k))
    folded = (w_qkv[0].astype(F32) * norm_gain[0].astype(F32)[None, :, None]).astype(BF)
    chunk = jnp.concatenate([folded[0], folded[1], folded[2], piece], axis=1)
    parts = gather_z(chunk, tp & 1)

    corner = {(0, 0): (0, 1), (0, 1): (1, 1), (1, 1): (1, 0), (1, 0): (0, 0)}
    turn = permute(hidden, lambda a, z, b, y, k: (*_at(corner, a, b, z), y, k))
    cross = permute(hidden, lambda a, z, b, y, k: (b, z, a, y, k) if a != b else None)
    own = jnp.where(same, hidden, turn)
    other = jnp.where(same, turn, cross)
    blocks = []
    for block in around(jnp.concatenate([own, other], axis=0)):
        blocks += [block, permute(block, swap_core)]

    ssq, ssq_send = call(
        squares_body,
        (shape((8, seg), F32), shape((8, seg), F32)),
        flops=4 * seg * 8 * feats * 8,
        nbytes=4 << 20,
        scalars=False,
    )(*blocks)
    ssq_got = permute(ssq_send, swap_hi)
    kv_send, q_send, weights, out_w = call(
        project_other_body,
        (
            shape((seg, 2 * hd), BF),
            shape((seg, hd), BF),
            shape((16 * hd, 3 * hd), BF),
            shape((16 * hd, hd), BF),
        ),
        flops=2 * seg * 8 * feats * 3 * hd,
        nbytes=8 << 20,
    )(pos, *blocks, *parts)
    kv_got = permute(kv_send, swap_hi)
    q_got = permute(q_send, swap_hi)
    own_part = call(
        project_own_body,
        shape((seg, 3 * hd), F32),
        flops=2 * seg * 8 * feats * 3 * hd,
        nbytes=8 << 20,
    )(pos, *blocks, weights)

    def combine(got, first):
        return call(
            lambda *refs: combine_body(*refs, features=16 * feats, first=first),
            shape(got.shape, BF),
            nbytes=1 << 20,
            scalars=False,
        )(own_part, got, ssq, ssq_got)

    kv = combine(kv_got, hd)
    q = combine(q_got, 0)
    prev = lax.ppermute(kv, "ctx", [(i, i + 1) for i in range(31)])
    e_own, sum_own = call(
        own_body,
        (shape((seg, seg), F32), shape((seg, hd), F32)),
        flops=2 * seg * seg * hd,
        nbytes=2 << 20,
        scalars=False,
    )(q, kv)
    attended = call(
        attend_body, shape((seg, hd), BF), flops=6 * seg * seg * hd, nbytes=2 << 20
    )(pos, q, kv, prev, e_own, sum_own)

    facing = permute(attended, lambda a, z, b, y, k: (a, z, 1 - b, y, k))
    out_w_other = permute(out_w, swap_hi)
    pieces = around(jnp.concatenate([attended, facing], axis=1))
    sizes = dict(flops=2 * seg * feats * 8 * hd, nbytes=3 << 20)
    out_send = call(output_other_body, shape((seg, feats), BF), **sizes)(
        pos, *pieces, out_w, out_w_other
    )
    out_got = permute(out_send, swap_core)
    out_own = call(output_own_body, shape((seg, feats), F32), **sizes)(
        pos, *pieces, out_w, out_w_other, hidden
    )
    return call(add_body, shape((seg, feats), BF), scalars=False)(out_own, out_got)


def _at(corner, a, b, z):
    to = corner[a, b]
    return to[0], z, to[1]


def solution(mesh):
    placed = (P("ctx", "tp"), P(None, "ctx"), P(None, None, "ctx", "tp"), P(None, "tp", "ctx"))
    return jax.shard_map(
        layer, mesh=mesh, in_specs=placed, out_specs=P("ctx", "tp"), check_vma=False
    )
```

```python
import math

import jax
import jax.numpy as jnp
from jax import lax
from jax.experimental import pallas as pl
from jax.experimental.pallas import tpu as pltpu
from jax.sharding import PartitionSpec as P


INTERPRET = False
AXES = ("ctx", "tp")
BF = jnp.bfloat16
F32 = jnp.float32
STEPS = ((0, -4, 4, 8), (2, 6), (-2, -6), (1, -3, 5, 9), (-1, -5, 3, 7))


def pairs_of(target):
    pairs = []
    for src in range(512):
        ctx, tp = divmod(src, 16)
        a, z, b, y, k = ctx // 16, ctx % 16, tp // 8, tp // 2 % 4, tp % 2
        to = target(a, z, b, y, k)
        if to is not None:
            a, z, b, y, k = to
            pairs.append((src, (a * 16 + z % 16) * 16 + b * 8 + y % 4 * 2 + k))
    return pairs


def permute(value, target):
    return lax.ppermute(value, AXES, pairs_of(target))


def call(body, outs, scratch=(), flops=0, nbytes=1 << 20, vmem=24 << 20, scalars=True):
    def run(*args):
        specs = [pl.BlockSpec(memory_space=pltpu.VMEM) for _ in args]
        if scalars:
            specs[0] = pl.BlockSpec(memory_space=pltpu.SMEM)
        return pl.pallas_call(
            body,
            out_shape=outs,
            in_specs=specs,
            out_specs=jax.tree.map(lambda _: pl.BlockSpec(memory_space=pltpu.VMEM), outs),
            scratch_shapes=list(scratch),
            compiler_params=pltpu.CompilerParams(vmem_limit_bytes=vmem),
            cost_estimate=pl.CostEstimate(flops=flops, bytes_accessed=nbytes, transcendentals=0),
            interpret=INTERPRET,
        )(*args)

    return run


def shape(dims, dtype):
    return jax.ShapeDtypeStruct(dims, dtype)


def place(pos):
    ctx, tp = pos[0], pos[1]
    return ctx >> 4, ctx & 15, tp >> 3, (tp >> 1) & 3, tp & 1


def gather_z(chunk, core):
    def move(value, by):
        return permute(value, lambda a, z, b, y, k: (a, z + by, b, y, k))

    up4 = move(chunk, 4)
    down4 = move(chunk, -4)
    relay = permute(
        jnp.where(core == 0, down4, up4), lambda a, z, b, y, k: (a, z + (4 if k else 12), b, y, k)
    )
    down2 = move(jnp.concatenate([chunk, down4], axis=0), -2)
    up2 = move(jnp.concatenate([chunk, up4], axis=0), 2)
    held = jnp.concatenate([chunk, up4, down4, relay], axis=0)
    down1 = move(held, -1)
    up1 = move(held, 1)
    return held, down2, up2, down1, up1


def squares_body(*refs):
    blocks, (own_ref, other_ref) = refs[:8], refs[8:]
    seg = own_ref.shape[1]
    ones = jnp.ones((own_ref.shape[0], blocks[0].shape[1]), BF)
    for first, ref in ((0, own_ref), (seg, other_ref)):
        total = jnp.zeros(ref.shape, F32)
        for block in blocks:
            wider = block[first : first + seg, :].astype(F32)
            total += lax.dot_general(
                ones,
                (wider * wider).astype(BF),
                (((1,), (1,)), ((), ())),
                preferred_element_type=F32,
            )
        ref[...] = total


def project_rows(pos, blocks, weights, first, seg):
    _, _, _, y, k = place(pos)
    rows = weights.shape[0] // 16
    tile = min(seg, 256)
    for r in range(0, seg, tile):
        acc = jnp.zeros((tile, weights.shape[1]), F32)
        for i in range(8):
            yy = (y + i // 2) & 3
            kk = k if i % 2 == 0 else 1 - k
            at = pl.multiple_of((yy * 2 + kk) * 2 * rows, 2 * rows)
            block = blocks[i][first + r : first + r + tile, :]
            acc += jnp.dot(block, weights[pl.ds(at, 2 * rows), :], preferred_element_type=F32)
        yield slice(r, r + tile), acc


EXTRA = 16


def project_other_body(pos, *refs):
    blocks, parts, ssq_ref, (kv_ref, q_ref, w_ref, out_w_ref) = (
        refs[:8], refs[8:13], refs[13], refs[14:],
    )
    _, z, _, _, _ = place(pos)
    rows = w_ref.shape[0] // 16
    seg, hd = q_ref.shape
    wide = w_ref.shape[1]
    for part, steps in zip(parts, STEPS):
        for i, step in enumerate(steps):
            at = pl.multiple_of(((z + step + 16) & 15) * rows, rows)
            w_ref[pl.ds(at, rows), :] = part[i * rows : (i + 1) * rows, :wide]
            out_w_ref[pl.ds(at, rows), :] = part[i * rows : (i + 1) * rows, wide:]
    for at, acc in project_rows(pos, blocks, w_ref, seg, seg):
        q_ref[at, :] = acc[:, :hd].astype(BF)
        kv_ref[at, :] = acc[:, hd:].astype(BF)
    half = kv_ref.shape[1]
    ssq = ssq_ref[:1, :]
    high = ssq.astype(BF).astype(F32)
    row = lax.broadcasted_iota(jnp.int32, (EXTRA, half), 0)
    extra = jnp.zeros((EXTRA, half), F32)
    for i, part in enumerate((high, ssq - high)):
        for j in range(seg // half):
            here = jnp.broadcast_to(part[:, j * half : (j + 1) * half], (EXTRA, half))
            extra = jnp.where(row == i * (seg // half) + j, here, extra)
    kv_ref[seg:, :] = extra.astype(BF)


def project_own_body(pos, *refs):
    blocks, (w_ref, own_ref) = refs[:8], refs[8:]
    for at, acc in project_rows(pos, blocks, w_ref, 0, own_ref.shape[0]):
        own_ref[at, :] = acc


def combine_body(own_ref, got_ref, ssq_ref, extra_ref, out_ref, *, features, first):
    seg, wide = out_ref.shape
    extra = extra_ref[seg:, :].astype(F32)
    parts = seg // extra.shape[1]
    got = [extra[j : j + 1, :] + extra[parts + j : parts + j + 1, :] for j in range(parts)]
    total = ssq_ref[...] + jnp.concatenate(got, axis=1)
    scale = lax.rsqrt(total * (1.0 / features) + 1e-06)
    column = lax.dot_general(
        scale,
        jnp.full((scale.shape[0], wide), 1.0 / scale.shape[0], F32),
        (((0,), (0,)), ((), ())),
        precision=lax.Precision.HIGHEST,
        preferred_element_type=F32,
    )
    own = own_ref[:, first : first + wide]
    out_ref[...] = ((own + got_ref[:seg, :].astype(F32)) * column).astype(BF)


def scores_of(q, keys):
    hd = q.shape[1]
    return lax.dot_general(
        q, keys, (((1,), (1,)), ((), ())), preferred_element_type=F32
    ) * (1.0 / math.sqrt(hd))


def own_body(q_ref, kv_ref, e_ref, sum_ref):
    hd = q_ref.shape[1]
    scores = scores_of(q_ref[...], kv_ref[:, :hd])
    row = lax.broadcasted_iota(jnp.int32, scores.shape, 0)
    col = lax.broadcasted_iota(jnp.int32, scores.shape, 1)
    e = jnp.where(col <= row, jnp.exp(scores), 0.0)
    e_ref[...] = e
    sum_ref[...] = jnp.broadcast_to(jnp.sum(e, axis=1, keepdims=True), sum_ref.shape)


def attend_body(pos, q_ref, kv_ref, prev_ref, e_ref, sum_ref, out_ref):
    hd = q_ref.shape[1]
    e = jnp.exp(scores_of(q_ref[...], prev_ref[:, :hd]))
    first = pos[0] == 0
    e = jnp.where(jnp.full(e.shape, first), 0.0, e)
    total = sum_ref[:, :1] + jnp.sum(e, axis=1, keepdims=True)
    inverse = 1.0 / total
    out = jnp.dot((e_ref[...] * inverse).astype(BF), kv_ref[:, hd:], preferred_element_type=F32)
    out += jnp.dot((e * inverse).astype(BF), prev_ref[:, hd:], preferred_element_type=F32)
    out_ref[...] = out.astype(BF)


def output_of(pos, pieces, w_ref, core):
    a, _, b, y, _ = place(pos)
    hd = w_ref.shape[1] // 2
    total = None
    for i in range(4):
        yy = (y + i) & 3
        at = pl.multiple_of(((core + 2 * yy + 2 * y) & 7) * 2 * hd, 2 * hd)
        both = w_ref[pl.ds(at, 2 * hd), :]
        own, other = both[:, :hd], both[:, hd:]
        same = jnp.full(own.shape, a == b)
        rows = []
        for half in (jnp.where(same, own, other), jnp.where(same, other, own)):
            rows.append(jnp.concatenate([half[:hd], half[hd:]], axis=1))
        part = jnp.dot(pieces[i][...], jnp.concatenate(rows, axis=0), preferred_element_type=F32)
        total = part if total is None else total + part
    return total


def output_other_body(pos, *refs):
    pieces, (w_ref, send_ref) = refs[:4], refs[4:]
    send_ref[...] = output_of(pos, pieces, w_ref, 1 - place(pos)[4]).astype(BF)


def output_own_body(pos, *refs):
    pieces, (w_ref, hidden_ref, out_ref) = refs[:4], refs[4:]
    core = place(pos)[4]
    out_ref[...] = hidden_ref[...].astype(F32) + output_of(pos, pieces, w_ref, core)


def add_body(own_ref, got_ref, out_ref):
    out_ref[...] = (own_ref[...] + got_ref[...].astype(F32)).astype(BF)


def swap_hi(a, z, b, y, k):
    return 1 - a, z, b, y, k


def swap_core(a, z, b, y, k):
    return a, z, b, y, 1 - k


def around(value):
    pieces = [value]
    for by in (1, 2, 3):
        pieces.append(permute(value, lambda a, z, b, y, k: (a, z, b, y - by, k)))
    return pieces


def layer(hidden, norm_gain, w_qkv, w_out):
    seg, feats = hidden.shape
    hd = w_out.shape[1]
    ctx, tp = lax.axis_index("ctx"), lax.axis_index("tp")
    pos = jnp.stack([ctx, tp]).astype(jnp.int32)
    same = (ctx >> 4) == (tp >> 3)

    piece_a = permute(w_out[0], lambda a, z, b, y, k: (b, z + 4 * y, a, z // 4, k))
    piece_b = permute(w_out[0], lambda a, z, b, y, k: (1 - b, z + 4 * y, a, z // 4, k))
    folded = (w_qkv[0].astype(F32) * norm_gain[0].astype(F32)[None, :, None]).astype(BF)
    chunk = jnp.concatenate([folded[0], folded[1], folded[2], piece_a, piece_b], axis=1)
    parts = gather_z(chunk, tp & 1)

    corner = {(0, 0): (0, 1), (0, 1): (1, 1), (1, 1): (1, 0), (1, 0): (0, 0)}
    turn = permute(hidden, lambda a, z, b, y, k: (*_at(corner, a, b, z), y, k))
    cross = permute(hidden, lambda a, z, b, y, k: (b, z, a, y, k) if a != b else None)
    own = jnp.where(same, hidden, turn)
    other = jnp.where(same, turn, cross)
    blocks = []
    for block in around(jnp.concatenate([own, other], axis=0)):
        blocks += [block, permute(block, swap_core)]

    ssq, ssq_send = call(
        squares_body,
        (shape((8, seg), F32), shape((8, seg), F32)),
        flops=4 * seg * 8 * feats * 8,
        nbytes=4 << 20,
        scalars=False,
    )(*blocks)
    kv_send, q_send, weights, out_w = call(
        project_other_body,
        (
            shape((seg + EXTRA, 2 * hd), BF),
            shape((seg, hd), BF),
            shape((16 * hd, 3 * hd), BF),
            shape((16 * hd, 2 * hd), BF),
        ),
        flops=2 * seg * 8 * feats * 3 * hd,
        nbytes=8 << 20,
    )(pos, *blocks, *parts, ssq_send)
    kv_got = permute(kv_send, swap_hi)
    q_got = permute(q_send, swap_hi)
    own_part = call(
        project_own_body,
        shape((seg, 3 * hd), F32),
        flops=2 * seg * 8 * feats * 3 * hd,
        nbytes=8 << 20,
    )(pos, *blocks, weights)

    def combine(got, first):
        return call(
            lambda *refs: combine_body(*refs, features=16 * feats, first=first),
            shape((seg, got.shape[1]), BF),
            nbytes=1 << 20,
            scalars=False,
        )(own_part, got, ssq, kv_got)

    kv = combine(kv_got, hd)
    q = combine(q_got, 0)
    prev = lax.ppermute(kv, "ctx", [(i, i + 1) for i in range(31)])
    e_own, sum_own = call(
        own_body,
        (shape((seg, seg), F32), shape((seg, hd), F32)),
        flops=2 * seg * seg * hd,
        nbytes=2 << 20,
        scalars=False,
    )(q, kv)
    attended = call(
        attend_body, shape((seg, hd), BF), flops=6 * seg * seg * hd, nbytes=2 << 20
    )(pos, q, kv, prev, e_own, sum_own)

    facing = permute(attended, lambda a, z, b, y, k: (a, z, 1 - b, y, k))
    pieces = around(jnp.concatenate([attended, facing], axis=1))
    sizes = dict(flops=2 * seg * feats * 8 * hd, nbytes=3 << 20)
    out_send = call(output_other_body, shape((seg, feats), BF), **sizes)(
        pos, *pieces, out_w
    )
    out_got = permute(out_send, swap_core)
    out_own = call(output_own_body, shape((seg, feats), F32), **sizes)(
        pos, *pieces, out_w, hidden
    )
    return call(add_body, shape((seg, feats), BF), scalars=False)(out_own, out_got)


def _at(corner, a, b, z):
    to = corner[a, b]
    return to[0], z, to[1]


def solution(mesh):
    placed = (P("ctx", "tp"), P(None, "ctx"), P(None, None, "ctx", "tp"), P(None, "tp", "ctx"))
    return jax.shard_map(
        layer, mesh=mesh, in_specs=placed, out_specs=P("ctx", "tp"), check_vma=False
    )
```

```python
import math

import jax
import jax.numpy as jnp
from jax import lax
from jax.experimental import pallas as pl
from jax.experimental.pallas import tpu as pltpu
from jax.sharding import PartitionSpec as P


INTERPRET = False
AXES = ("ctx", "tp")
BF = jnp.bfloat16
F32 = jnp.float32
STEPS = ((0, -4, 4, 8), (2, 6), (-2, -6), (1, -3, 5, 9), (-1, -5, 3, 7))


def pairs_of(target):
    pairs = []
    for src in range(512):
        ctx, tp = divmod(src, 16)
        a, z, b, y, k = ctx // 16, ctx % 16, tp // 8, tp // 2 % 4, tp % 2
        to = target(a, z, b, y, k)
        if to is not None:
            a, z, b, y, k = to
            pairs.append((src, (a * 16 + z % 16) * 16 + b * 8 + y % 4 * 2 + k))
    return pairs


def permute(value, target):
    return lax.ppermute(value, AXES, pairs_of(target))


def call(body, outs, scratch=(), flops=0, nbytes=1 << 20, vmem=24 << 20, scalars=True):
    def run(*args):
        specs = [pl.BlockSpec(memory_space=pltpu.VMEM) for _ in args]
        if scalars:
            specs[0] = pl.BlockSpec(memory_space=pltpu.SMEM)
        return pl.pallas_call(
            body,
            out_shape=outs,
            in_specs=specs,
            out_specs=jax.tree.map(lambda _: pl.BlockSpec(memory_space=pltpu.VMEM), outs),
            scratch_shapes=list(scratch),
            compiler_params=pltpu.CompilerParams(vmem_limit_bytes=vmem),
            cost_estimate=pl.CostEstimate(flops=flops, bytes_accessed=nbytes, transcendentals=0),
            interpret=INTERPRET,
        )(*args)

    return run


def shape(dims, dtype):
    return jax.ShapeDtypeStruct(dims, dtype)


def place(pos):
    ctx, tp = pos[0], pos[1]
    return ctx >> 4, ctx & 15, tp >> 3, (tp >> 1) & 3, tp & 1


def gather_z(chunk, core):
    def move(value, by):
        return permute(value, lambda a, z, b, y, k: (a, z + by, b, y, k))

    up4 = move(chunk, 4)
    down4 = move(chunk, -4)
    relay = permute(
        jnp.where(core == 0, down4, up4), lambda a, z, b, y, k: (a, z + (4 if k else 12), b, y, k)
    )
    down2 = move(jnp.concatenate([chunk, down4], axis=0), -2)
    up2 = move(jnp.concatenate([chunk, up4], axis=0), 2)
    held = jnp.concatenate([chunk, up4, down4, relay], axis=0)
    down1 = move(held, -1)
    up1 = move(held, 1)
    return held, down2, up2, down1, up1


def squares_body(*refs):
    blocks, (own_ref, other_ref) = refs[:8], refs[8:]
    seg = own_ref.shape[1]
    ones = jnp.ones((own_ref.shape[0], blocks[0].shape[1]), BF)
    for first, ref in ((0, own_ref), (seg, other_ref)):
        total = jnp.zeros(ref.shape, F32)
        for block in blocks:
            wider = block[first : first + seg, :].astype(F32)
            total += lax.dot_general(
                ones,
                (wider * wider).astype(BF),
                (((1,), (1,)), ((), ())),
                preferred_element_type=F32,
            )
        ref[...] = total


def project_rows(pos, blocks, weights, first, seg):
    _, _, _, y, k = place(pos)
    rows = weights.shape[0] // 16
    tile = min(seg, 256)
    for r in range(0, seg, tile):
        acc = jnp.zeros((tile, weights.shape[1]), F32)
        for i in range(8):
            yy = (y + i // 2) & 3
            kk = k if i % 2 == 0 else 1 - k
            at = pl.multiple_of((yy * 2 + kk) * 2 * rows, 2 * rows)
            block = blocks[i][first + r : first + r + tile, :]
            acc += jnp.dot(block, weights[pl.ds(at, 2 * rows), :], preferred_element_type=F32)
        yield slice(r, r + tile), acc


EXTRA = 16


def project_other_body(pos, *refs):
    blocks, parts, ssq_ref, (kv_ref, q_ref, w_ref, out_w_ref) = (
        refs[:8], refs[8:13], refs[13], refs[14:],
    )
    _, z, _, _, _ = place(pos)
    rows = w_ref.shape[0] // 16
    seg, hd = q_ref.shape
    wide = w_ref.shape[1]
    for part, steps in zip(parts, STEPS):
        for i, step in enumerate(steps):
            at = pl.multiple_of(((z + step + 16) & 15) * rows, rows)
            w_ref[pl.ds(at, rows), :] = part[i * rows : (i + 1) * rows, :wide]
            out_w_ref[pl.ds(at, rows), :] = part[i * rows : (i + 1) * rows, wide:]
    for at, acc in project_rows(pos, blocks, w_ref, seg, seg):
        q_ref[at, :] = acc[:, :hd].astype(BF)
        kv_ref[at, :] = acc[:, hd:].astype(BF)
    half = kv_ref.shape[1]
    ssq = ssq_ref[:1, :]
    high = ssq.astype(BF).astype(F32)
    row = lax.broadcasted_iota(jnp.int32, (EXTRA, half), 0)
    extra = jnp.zeros((EXTRA, half), F32)
    for i, part in enumerate((high, ssq - high)):
        for j in range(seg // half):
            here = jnp.broadcast_to(part[:, j * half : (j + 1) * half], (EXTRA, half))
            extra = jnp.where(row == i * (seg // half) + j, here, extra)
    kv_ref[seg:, :] = extra.astype(BF)


def project_own_body(pos, *refs):
    blocks, (w_ref, own_ref) = refs[:8], refs[8:]
    for at, acc in project_rows(pos, blocks, w_ref, 0, own_ref.shape[0]):
        own_ref[at, :] = acc


def combine_body(own_ref, got_ref, ssq_ref, extra_ref, out_ref, *, features, first):
    seg, wide = out_ref.shape
    extra = extra_ref[seg:, :].astype(F32)
    parts = seg // extra.shape[1]
    got = [extra[j : j + 1, :] + extra[parts + j : parts + j + 1, :] for j in range(parts)]
    total = ssq_ref[...] + jnp.concatenate(got, axis=1)
    scale = lax.rsqrt(total * (1.0 / features) + 1e-06)
    column = lax.dot_general(
        scale,
        jnp.full((scale.shape[0], wide), 1.0 / scale.shape[0], F32),
        (((0,), (0,)), ((), ())),
        precision=lax.Precision.HIGHEST,
        preferred_element_type=F32,
    )
    own = own_ref[:, first : first + wide]
    out_ref[...] = ((own + got_ref[:seg, :].astype(F32)) * column).astype(BF)


def scores_of(q, keys):
    hd = q.shape[1]
    return lax.dot_general(
        q, keys, (((1,), (1,)), ((), ())), preferred_element_type=F32
    ) * (1.0 / math.sqrt(hd))


def own_body(q_ref, kv_ref, e_ref, sum_ref):
    hd = q_ref.shape[1]
    scores = scores_of(q_ref[...], kv_ref[:, :hd])
    row = lax.broadcasted_iota(jnp.int32, scores.shape, 0)
    col = lax.broadcasted_iota(jnp.int32, scores.shape, 1)
    e = jnp.where(col <= row, jnp.exp(scores), 0.0)
    e_ref[...] = e
    sum_ref[...] = jnp.broadcast_to(jnp.sum(e, axis=1, keepdims=True), sum_ref.shape)


def attend_body(pos, q_ref, kv_ref, prev_ref, e_ref, sum_ref, out_ref):
    hd = q_ref.shape[1]
    e = jnp.exp(scores_of(q_ref[...], prev_ref[:, :hd]))
    first = pos[0] == 0
    e = jnp.where(jnp.full(e.shape, first), 0.0, e)
    total = sum_ref[:, :1] + jnp.sum(e, axis=1, keepdims=True)
    inverse = 1.0 / total
    out = jnp.dot((e_ref[...] * inverse).astype(BF), kv_ref[:, hd:], preferred_element_type=F32)
    out += jnp.dot((e * inverse).astype(BF), prev_ref[:, hd:], preferred_element_type=F32)
    out_ref[...] = out.astype(BF)


def output_of(pos, pieces, w_own, w_other, core):
    a, _, b, y, _ = place(pos)
    hd = w_own.shape[1]
    total = None
    for i in range(4):
        yy = (y + i) & 3
        at = pl.multiple_of(((core + 2 * yy + 2 * y) & 7) * 2 * hd, 2 * hd)
        own = w_own[pl.ds(at, 2 * hd), :]
        other = w_other[pl.ds(at, 2 * hd), :]
        same = jnp.full(own.shape, a == b)
        rows = []
        for both in (jnp.where(same, own, other), jnp.where(same, other, own)):
            rows.append(jnp.concatenate([both[:hd], both[hd:]], axis=1))
        part = jnp.dot(pieces[i][...], jnp.concatenate(rows, axis=0), preferred_element_type=F32)
        total = part if total is None else total + part
    return total


def output_other_body(pos, *refs):
    pieces, (w_own, w_other, send_ref) = refs[:4], refs[4:]
    core = 1 - place(pos)[4]
    send_ref[...] = output_of(pos, pieces, w_own, w_other, core).astype(BF)


def output_own_body(pos, *refs):
    pieces, (w_own, w_other, hidden_ref, out_ref) = refs[:4], refs[4:]
    core = place(pos)[4]
    out_ref[...] = hidden_ref[...].astype(F32) + output_of(pos, pieces, w_own, w_other, core)


def add_body(own_ref, got_ref, out_ref):
    out_ref[...] = (own_ref[...] + got_ref[...].astype(F32)).astype(BF)


def swap_hi(a, z, b, y, k):
    return 1 - a, z, b, y, k


def swap_core(a, z, b, y, k):
    return a, z, b, y, 1 - k


def around(value):
    pieces = [value]
    for by in (1, 2, 3):
        pieces.append(permute(value, lambda a, z, b, y, k: (a, z, b, y - by, k)))
    return pieces


def layer(hidden, norm_gain, w_qkv, w_out):
    seg, feats = hidden.shape
    hd = w_out.shape[1]
    ctx, tp = lax.axis_index("ctx"), lax.axis_index("tp")
    pos = jnp.stack([ctx, tp]).astype(jnp.int32)
    same = (ctx >> 4) == (tp >> 3)

    piece = permute(w_out[0], lambda a, z, b, y, k: (b, z + 4 * y, a, z // 4, k))
    folded = (w_qkv[0].astype(F32) * norm_gain[0].astype(F32)[None, :, None]).astype(BF)
    chunk = jnp.concatenate([folded[0], folded[1], folded[2], piece], axis=1)
    parts = gather_z(chunk, tp & 1)

    corner = {(0, 0): (0, 1), (0, 1): (1, 1), (1, 1): (1, 0), (1, 0): (0, 0)}
    turn = permute(hidden, lambda a, z, b, y, k: (*_at(corner, a, b, z), y, k))
    cross = permute(hidden, lambda a, z, b, y, k: (b, z, a, y, k) if a != b else None)
    own = jnp.where(same, hidden, turn)
    other = jnp.where(same, turn, cross)
    blocks = []
    for block in around(jnp.concatenate([own, other], axis=0)):
        blocks += [block, permute(block, swap_core)]

    ssq, ssq_send = call(
        squares_body,
        (shape((8, seg), F32), shape((8, seg), F32)),
        flops=4 * seg * 8 * feats * 8,
        nbytes=4 << 20,
        scalars=False,
    )(*blocks)
    kv_send, q_send, weights, out_w = call(
        project_other_body,
        (
            shape((seg + EXTRA, 2 * hd), BF),
            shape((seg, hd), BF),
            shape((16 * hd, 3 * hd), BF),
            shape((16 * hd, hd), BF),
        ),
        flops=2 * seg * 8 * feats * 3 * hd,
        nbytes=8 << 20,
    )(pos, *blocks, *parts, ssq_send)
    kv_got = permute(kv_send, swap_hi)
    q_got = permute(q_send, swap_hi)
    own_part = call(
        project_own_body,
        shape((seg, 3 * hd), F32),
        flops=2 * seg * 8 * feats * 3 * hd,
        nbytes=8 << 20,
    )(pos, *blocks, weights)

    def combine(got, first):
        return call(
            lambda *refs: combine_body(*refs, features=16 * feats, first=first),
            shape((seg, got.shape[1]), BF),
            nbytes=1 << 20,
            scalars=False,
        )(own_part, got, ssq, kv_got)

    kv = combine(kv_got, hd)
    q = combine(q_got, 0)
    prev = lax.ppermute(kv, "ctx", [(i, i + 1) for i in range(31)])
    e_own, sum_own = call(
        own_body,
        (shape((seg, seg), F32), shape((seg, hd), F32)),
        flops=2 * seg * seg * hd,
        nbytes=2 << 20,
        scalars=False,
    )(q, kv)
    attended = call(
        attend_body, shape((seg, hd), BF), flops=6 * seg * seg * hd, nbytes=2 << 20
    )(pos, q, kv, prev, e_own, sum_own)

    facing = permute(attended, lambda a, z, b, y, k: (a, z, 1 - b, y, k))
    out_w_other = permute(out_w, swap_hi)
    pieces = around(jnp.concatenate([attended, facing], axis=1))
    sizes = dict(flops=2 * seg * feats * 8 * hd, nbytes=3 << 20)
    out_send = call(output_other_body, shape((seg, feats), BF), **sizes)(
        pos, *pieces, out_w, out_w_other
    )
    out_got = permute(out_send, swap_core)
    out_own = call(output_own_body, shape((seg, feats), F32), **sizes)(
        pos, *pieces, out_w, out_w_other, hidden
    )
    return call(add_body, shape((seg, feats), BF), scalars=False)(out_own, out_got)


def _at(corner, a, b, z):
    to = corner[a, b]
    return to[0], z, to[1]


def solution(mesh):
    placed = (P("ctx", "tp"), P(None, "ctx"), P(None, None, "ctx", "tp"), P(None, "tp", "ctx"))
    return jax.shard_map(
        layer, mesh=mesh, in_specs=placed, out_specs=P("ctx", "tp"), check_vma=False
    )
```

```python
import math

import jax
import jax.numpy as jnp
from jax import lax
from jax.experimental import pallas as pl
from jax.experimental.pallas import tpu as pltpu
from jax.sharding import PartitionSpec as P


INTERPRET = False
AXES = ("ctx", "tp")
BF = jnp.bfloat16
F32 = jnp.float32
HELD = (0, -4, 4, 8)


def pairs_of(target):
    pairs = []
    for src in range(512):
        ctx, tp = divmod(src, 16)
        a, z, b, y, k = ctx // 16, ctx % 16, tp // 8, tp // 2 % 4, tp % 2
        to = target(a, z, b, y, k)
        if to is not None:
            a, z, b, y, k = to
            pairs.append((src, (a * 16 + z % 16) * 16 + b * 8 + y % 4 * 2 + k))
    return pairs


def permute(value, target):
    return lax.ppermute(value, AXES, pairs_of(target))


def call(body, outs, scratch=(), flops=0, nbytes=1 << 20, vmem=24 << 20, scalars=True):
    def run(*args):
        specs = [pl.BlockSpec(memory_space=pltpu.VMEM) for _ in args]
        if scalars:
            specs[0] = pl.BlockSpec(memory_space=pltpu.SMEM)
        return pl.pallas_call(
            body,
            out_shape=outs,
            in_specs=specs,
            out_specs=jax.tree.map(lambda _: pl.BlockSpec(memory_space=pltpu.VMEM), outs),
            scratch_shapes=list(scratch),
            compiler_params=pltpu.CompilerParams(vmem_limit_bytes=vmem),
            cost_estimate=pl.CostEstimate(flops=flops, bytes_accessed=nbytes, transcendentals=0),
            interpret=INTERPRET,
        )(*args)

    return run


def shape(dims, dtype):
    return jax.ShapeDtypeStruct(dims, dtype)


def place(pos):
    ctx, tp = pos[0], pos[1]
    return ctx >> 4, ctx & 15, tp >> 3, (tp >> 1) & 3, tp & 1


def gather_z(chunk, core):
    def move(value, by):
        return permute(value, lambda a, z, b, y, k: (a, z + by, b, y, k))

    up4 = move(chunk, 4)
    down4 = move(chunk, -4)
    relay = permute(
        jnp.where(core == 0, down4, up4), lambda a, z, b, y, k: (a, z + (4 if k else 12), b, y, k)
    )
    held = jnp.concatenate([chunk, up4, down4, relay], axis=0)
    two = permute(held, lambda a, z, b, y, k: (a, z + (2 if k else 14), b, y, k))
    return held, two, move(held, -1), move(held, 1)


def columns_of(blocks, i, first, size):
    if i % 2 == 0:
        return blocks[i // 2][first : first + size, :]
    if i > 1:
        first += (i // 2 - 1) * blocks[0].shape[0]
    return blocks[4 if i == 1 else 5][first : first + size, :]


def squares_body(*refs):
    blocks, (own_ref, other_ref) = refs[:6], refs[6:]
    seg = own_ref.shape[1]
    ones = jnp.ones((own_ref.shape[0], blocks[0].shape[1]), BF)
    for first, ref in ((0, own_ref), (seg, other_ref)):
        total = jnp.zeros(ref.shape, F32)
        for i in range(8):
            wider = columns_of(blocks, i, first, seg).astype(F32)
            total += lax.dot_general(
                ones,
                (wider * wider).astype(BF),
                (((1,), (1,)), ((), ())),
                preferred_element_type=F32,
            )
        ref[...] = total


def project_rows(pos, blocks, weights, first, seg):
    _, _, _, y, k = place(pos)
    rows = weights.shape[0] // 16
    tile = min(seg, 256)
    for r in range(0, seg, tile):
        acc = jnp.zeros((tile, weights.shape[1]), F32)
        for i in range(8):
            yy = (y + i // 2) & 3
            kk = k if i % 2 == 0 else 1 - k
            at = pl.multiple_of((yy * 2 + kk) * 2 * rows, 2 * rows)
            block = columns_of(blocks, i, first + r, tile)
            acc += jnp.dot(block, weights[pl.ds(at, 2 * rows), :], preferred_element_type=F32)
        yield slice(r, r + tile), acc


EXTRA = 16


def project_other_body(pos, *refs):
    blocks, parts, ssq_ref, (kv_ref, q_ref, w_ref, out_w_ref) = (
        refs[:6], refs[6:10], refs[10], refs[11:],
    )
    _, z, _, _, k = place(pos)
    rows = w_ref.shape[0] // 16
    seg, hd = q_ref.shape
    wide = w_ref.shape[1]
    for part, base in zip(parts, (0, 2 - 4 * k, 1, -1)):
        for i, step in enumerate(HELD):
            at = pl.multiple_of(((z + base + step + 16) & 15) * rows, rows)
            w_ref[pl.ds(at, rows), :] = part[i * rows : (i + 1) * rows, :wide]
            out_w_ref[pl.ds(at, rows), :] = part[i * rows : (i + 1) * rows, wide:]
    for at, acc in project_rows(pos, blocks, w_ref, seg, seg):
        q_ref[at, :] = acc[:, :hd].astype(BF)
        kv_ref[at, :] = acc[:, hd:].astype(BF)
    half = kv_ref.shape[1]
    ssq = ssq_ref[:1, :]
    high = ssq.astype(BF).astype(F32)
    row = lax.broadcasted_iota(jnp.int32, (EXTRA, half), 0)
    extra = jnp.zeros((EXTRA, half), F32)
    for i, part in enumerate((high, ssq - high)):
        for j in range(seg // half):
            here = jnp.broadcast_to(part[:, j * half : (j + 1) * half], (EXTRA, half))
            extra = jnp.where(row == i * (seg // half) + j, here, extra)
    kv_ref[seg:, :] = extra.astype(BF)


def project_own_body(pos, *refs):
    blocks, (w_ref, own_ref) = refs[:6], refs[6:]
    for at, acc in project_rows(pos, blocks, w_ref, 0, own_ref.shape[0]):
        own_ref[at, :] = acc


def combine_body(own_ref, got_ref, ssq_ref, extra_ref, out_ref, *, features, first):
    seg, wide = out_ref.shape
    extra = extra_ref[seg:, :].astype(F32)
    parts = seg // extra.shape[1]
    got = [extra[j : j + 1, :] + extra[parts + j : parts + j + 1, :] for j in range(parts)]
    total = ssq_ref[...] + jnp.concatenate(got, axis=1)
    scale = lax.rsqrt(total * (1.0 / features) + 1e-06)
    column = lax.dot_general(
        scale,
        jnp.full((scale.shape[0], wide), 1.0 / scale.shape[0], F32),
        (((0,), (0,)), ((), ())),
        precision=lax.Precision.HIGHEST,
        preferred_element_type=F32,
    )
    own = own_ref[:, first : first + wide]
    out_ref[...] = ((own + got_ref[:seg, :].astype(F32)) * column).astype(BF)


def scores_of(q, keys):
    hd = q.shape[1]
    return lax.dot_general(
        q, keys, (((1,), (1,)), ((), ())), preferred_element_type=F32
    ) * (1.0 / math.sqrt(hd))


def own_body(q_ref, kv_ref, e_ref, sum_ref):
    hd = q_ref.shape[1]
    scores = scores_of(q_ref[...], kv_ref[:, :hd])
    row = lax.broadcasted_iota(jnp.int32, scores.shape, 0)
    col = lax.broadcasted_iota(jnp.int32, scores.shape, 1)
    e = jnp.where(col <= row, jnp.exp(scores), 0.0)
    e_ref[...] = e
    sum_ref[...] = jnp.broadcast_to(jnp.sum(e, axis=1, keepdims=True), sum_ref.shape)


def attend_body(pos, q_ref, kv_ref, prev_ref, e_ref, sum_ref, out_ref):
    hd = q_ref.shape[1]
    e = jnp.exp(scores_of(q_ref[...], prev_ref[:, :hd]))
    first = pos[0] == 0
    e = jnp.where(jnp.full(e.shape, first), 0.0, e)
    total = sum_ref[:, :1] + jnp.sum(e, axis=1, keepdims=True)
    inverse = 1.0 / total
    out = jnp.dot((e_ref[...] * inverse).astype(BF), kv_ref[:, hd:], preferred_element_type=F32)
    out += jnp.dot((e * inverse).astype(BF), prev_ref[:, hd:], preferred_element_type=F32)
    out_ref[...] = out.astype(BF)


def output_of(pos, pieces, w_own, w_other, core):
    a, _, b, y, _ = place(pos)
    hd = w_own.shape[1]
    total = None
    for i in range(4):
        yy = (y + i) & 3
        at = pl.multiple_of(((core + 2 * yy + 2 * y) & 7) * 2 * hd, 2 * hd)
        own = w_own[pl.ds(at, 2 * hd), :]
        other = w_other[pl.ds(at, 2 * hd), :]
        same = jnp.full(own.shape, a == b)
        rows = []
        for both in (jnp.where(same, own, other), jnp.where(same, other, own)):
            rows.append(jnp.concatenate([both[:hd], both[hd:]], axis=1))
        part = jnp.dot(pieces[i][...], jnp.concatenate(rows, axis=0), preferred_element_type=F32)
        total = part if total is None else total + part
    return total


def output_other_body(pos, *refs):
    pieces, (w_own, w_other, send_ref) = refs[:4], refs[4:]
    core = 1 - place(pos)[4]
    send_ref[...] = output_of(pos, pieces, w_own, w_other, core).astype(BF)


def output_own_body(pos, *refs):
    pieces, (w_own, w_other, hidden_ref, out_ref) = refs[:4], refs[4:]
    core = place(pos)[4]
    out_ref[...] = hidden_ref[...].astype(F32) + output_of(pos, pieces, w_own, w_other, core)


def add_body(own_ref, got_ref, out_ref):
    out_ref[...] = (own_ref[...] + got_ref[...].astype(F32)).astype(BF)


def swap_hi(a, z, b, y, k):
    return 1 - a, z, b, y, k


def swap_core(a, z, b, y, k):
    return a, z, b, y, 1 - k


def around(value):
    pieces = [value]
    for by in (1, 2, 3):
        pieces.append(permute(value, lambda a, z, b, y, k: (a, z, b, y - by, k)))
    return pieces


def layer(hidden, norm_gain, w_qkv, w_out):
    seg, feats = hidden.shape
    hd = w_out.shape[1]
    ctx, tp = lax.axis_index("ctx"), lax.axis_index("tp")
    pos = jnp.stack([ctx, tp]).astype(jnp.int32)
    same = (ctx >> 4) == (tp >> 3)

    piece = permute(w_out[0], lambda a, z, b, y, k: (b, z + 4 * y, a, z // 4, k))
    folded = (w_qkv[0].astype(F32) * norm_gain[0].astype(F32)[None, :, None]).astype(BF)
    chunk = jnp.concatenate([folded[0], folded[1], folded[2], piece], axis=1)
    parts = gather_z(chunk, tp & 1)

    corner = {(0, 0): (0, 1), (0, 1): (1, 1), (1, 1): (1, 0), (1, 0): (0, 0)}
    turn = permute(hidden, lambda a, z, b, y, k: (*_at(corner, a, b, z), y, k))
    cross = permute(hidden, lambda a, z, b, y, k: (b, z, a, y, k) if a != b else None)
    own = jnp.where(same, hidden, turn)
    other = jnp.where(same, turn, cross)
    blocks = around(jnp.concatenate([own, other], axis=0))
    blocks += [
        permute(blocks[0], swap_core), permute(jnp.concatenate(blocks[1:], axis=0), swap_core)
    ]

    ssq, ssq_send = call(
        squares_body,
        (shape((8, seg), F32), shape((8, seg), F32)),
        flops=4 * seg * 8 * feats * 8,
        nbytes=4 << 20,
        scalars=False,
    )(*blocks)
    kv_send, q_send, weights, out_w = call(
        project_other_body,
        (
            shape((seg + EXTRA, 2 * hd), BF),
            shape((seg, hd), BF),
            shape((16 * hd, 3 * hd), BF),
            shape((16 * hd, hd), BF),
        ),
        flops=2 * seg * 8 * feats * 3 * hd,
        nbytes=8 << 20,
    )(pos, *blocks, *parts, ssq_send)
    kv_got = permute(kv_send, swap_hi)
    q_got = permute(q_send, swap_hi)
    own_part = call(
        project_own_body,
        shape((seg, 3 * hd), F32),
        flops=2 * seg * 8 * feats * 3 * hd,
        nbytes=8 << 20,
    )(pos, *blocks, weights)

    def combine(got, first):
        return call(
            lambda *refs: combine_body(*refs, features=16 * feats, first=first),
            shape((seg, got.shape[1]), BF),
            nbytes=1 << 20,
            scalars=False,
        )(own_part, got, ssq, kv_got)

    kv = combine(kv_got, hd)
    q = combine(q_got, 0)
    prev = lax.ppermute(kv, "ctx", [(i, i + 1) for i in range(31)])
    e_own, sum_own = call(
        own_body,
        (shape((seg, seg), F32), shape((seg, hd), F32)),
        flops=2 * seg * seg * hd,
        nbytes=2 << 20,
        scalars=False,
    )(q, kv)
    attended = call(
        attend_body, shape((seg, hd), BF), flops=6 * seg * seg * hd, nbytes=2 << 20
    )(pos, q, kv, prev, e_own, sum_own)

    facing = permute(attended, lambda a, z, b, y, k: (a, z, 1 - b, y, k))
    out_w_other = permute(out_w, swap_hi)
    pieces = around(jnp.concatenate([attended, facing], axis=1))
    sizes = dict(flops=2 * seg * feats * 8 * hd, nbytes=3 << 20)
    out_send = call(output_other_body, shape((seg, feats), BF), **sizes)(
        pos, *pieces, out_w, out_w_other
    )
    out_got = permute(out_send, swap_core)
    out_own = call(output_own_body, shape((seg, feats), F32), **sizes)(
        pos, *pieces, out_w, out_w_other, hidden
    )
    return call(add_body, shape((seg, feats), BF), scalars=False)(out_own, out_got)


def _at(corner, a, b, z):
    to = corner[a, b]
    return to[0], z, to[1]


def solution(mesh):
    placed = (P("ctx", "tp"), P(None, "ctx"), P(None, None, "ctx", "tp"), P(None, "tp", "ctx"))
    return jax.shard_map(
        layer, mesh=mesh, in_specs=placed, out_specs=P("ctx", "tp"), check_vma=False
    )
```
